256 devices in a mesh: cluster: 4 (over x), sub: 64 (over y, z, core).
Axes of the slice: x: 4, y: 4, z: 8, core: 2. Of those that a mesh axis runs over, the one named last changes fastest.
Arguments:
- dual_ops: float32 [262144, 1024], P(('cluster', 'sub')), may hold values from -21 to 21, as said below
- boundary_solve_blocks: float32 [262144, 1024], P(('cluster', 'sub')), may hold values from -21 to 21, as said below
- rigid_images: float32 [1536, 1024], P(('cluster', 'sub')), may hold values from -0.1875 to 0.1875
- coarse_rows: float32 [1536, 1536], P(('cluster', 'sub')), may hold values from -1.5 to 1.5, as said below
- gap_raw: float32 [262144, 256], P(('cluster', 'sub')), may hold values from -12 to 12
- row_maps: int32 [256, 2, 128], P(('cluster', 'sub')), may hold values from 0 to 1023, as said below
Outputs:
- multipliers: float32 [262144, 256], P(('cluster', 'sub'))
- residual: float32 [262144, 256], P(('cluster', 'sub'))
- norms: float32 [2, 256], replicated
The draws below stay inside these ranges and needn't reach their ends.
Inputs may be any that keep to these rules, and one draw needn't show every extreme that they name: `row_maps`: A subdomain's 2 * 128 row numbers all differ; its second list faces the first list of the next subdomain, row by row. `dual_ops`: each block of a subdomain is symmetric positive definite. `boundary_solve_blocks`: each block of a subdomain is symmetric positive definite. `coarse_rows`: Symmetric.
All inputs are finite; a program needn't handle non-finite values.
Results may differ from the reference program's by a relative error of at most 0.0003.
Values sent between devices are 32-bit elements; how exact they have to be, the bound alone decides.
No kernel may reach another device: no remote copies, remote signals or barrier semaphores. Data moves between devices by JAX's collectives and lax.ppermute only.
A program may use at most 64 MiB of HBM per device.

```python
import math
import jax
import jax.numpy as jnp
from jax import lax

M = 1024
P_SIZE = 128
MODES = 6
R = 256
ITERS = 2
SUBS = 256
COARSE = 1536


def spd_blocks(key, low_diag, high_diag, spread, off_weight):
    first_key, second_key, third_key = jax.random.split(key, 3)
    noise = jax.random.uniform(first_key, (SUBS, M, M), jnp.float32, -1.0, 1.0)
    symmetric = 0.5 * (noise + jnp.swapaxes(noise, 1, 2))
    row_ids = lax.broadcasted_iota(jnp.int32, (M, M), 0)
    col_ids = lax.broadcasted_iota(jnp.int32, (M, M), 1)
    on_diag = (row_ids == col_ids)[None, :, :]
    diagonal = jax.random.uniform(second_key, (SUBS, M, 1), jnp.float32, low_diag, high_diag)
    scales = jnp.exp(jax.random.uniform(third_key, (SUBS, M), jnp.float32, 0.0, math.log(spread)))
    off_scale = off_weight / math.sqrt(M)
    core = jnp.where(on_diag, diagonal, off_scale * symmetric)
    block = core * scales[:, :, None] * scales[:, None, :]
    return block.reshape(SUBS * M, M)


def draw_dual_ops(key, part):
    key = jax.random.fold_in(key, 11)
    return spd_blocks(key, 1.0, 2.0, 3.2, 0.75)


def draw_boundary_solve_blocks(key, part):
    key = jax.random.fold_in(key, 23)
    return spd_blocks(key, 1.0, 2.0, 3.2, 0.75)


def draw_coarse_rows(key, part):
    first_key, second_key = jax.random.split(jax.random.fold_in(key, 31))
    noise = jax.random.uniform(first_key, (COARSE, COARSE), jnp.float32, -1.0, 1.0)
    symmetric = 0.5 * (noise + noise.T)
    row_ids = lax.broadcasted_iota(jnp.int32, (COARSE, COARSE), 0)
    col_ids = lax.broadcasted_iota(jnp.int32, (COARSE, COARSE), 1)
    distance = jnp.abs(row_ids // MODES - col_ids // MODES).astype(jnp.float32)
    reach = 0.25
    diagonal = jax.random.uniform(second_key, (COARSE, 1), jnp.float32, 0.5, 1.5)
    envelope = reach * jnp.exp(-4.0 * distance / SUBS)
    return jnp.where(row_ids == col_ids, diagonal, envelope * symmetric)


def draw_gap_raw(key, part):
    first_key = jax.random.fold_in(jax.random.fold_in(key, 41), 0)
    place = (lax.broadcasted_iota(jnp.int32, (SUBS * M, 1), 0) // M).astype(jnp.float32)
    values = jax.random.truncated_normal(first_key, -4.0, 4.0, (SUBS * M, R), jnp.float32)
    return values * (1.0 + 2.0 * place / (SUBS - 1))


def one_map(device_key):
    return jax.random.permutation(device_key, M)[:2 * P_SIZE].reshape(2, P_SIZE).astype(jnp.int32)


def draw_row_maps(key, part):
    device_keys = jax.random.split(jax.random.fold_in(key, 51), SUBS)
    return jax.vmap(one_map)(device_keys)


def levels(stream_key, extent, shards, least, high):
    loudness = 1.0
    for axis_at, shards_of in shards:
        steps = jax.random.uniform(jax.random.fold_in(jax.random.fold_in(stream_key, 6), axis_at), (shards_of,), jnp.float32, least / len(shards), high / len(shards))
        loudness = loudness * jnp.repeat(jnp.exp(steps), extent[axis_at] // shards_of).reshape((-1,) + (1,) * (len(extent) - 1 - axis_at))
    return loudness


def bell_draw(stream_key, shape, deviation, most, cuts=(), dtype=jnp.bfloat16):
    entries = jax.random.normal(stream_key, shape, jnp.float32) * deviation
    if len(cuts) > 0:
        entries = levels(stream_key, shape, cuts, -0.22, 0.18) * entries
    return jnp.clip(entries, min=-most, max=most).astype(dtype)


def setup_inputs(seed: int = 0) -> dict:
    seeds = jax.random.split(jax.random.key(seed), 7)
    dual_ops = draw_dual_ops(jax.random.fold_in(seeds[6], 71), 0)
    boundary_solve_blocks = draw_boundary_solve_blocks(jax.random.fold_in(seeds[6], 71), 0)
    rigid_images = bell_draw(seeds[2], (COARSE, M), M ** -0.5, 0.1875, ((0, 256),), jnp.float32)
    coarse_rows = draw_coarse_rows(jax.random.fold_in(seeds[6], 71), 0)
    gap_raw = draw_gap_raw(jax.random.fold_in(seeds[6], 71), 0)
    row_maps = draw_row_maps(jax.random.fold_in(seeds[6], 71), 0)
    return dict(dual_ops=dual_ops, boundary_solve_blocks=boundary_solve_blocks, rigid_images=rigid_images, coarse_rows=coarse_rows, gap_raw=gap_raw, row_maps=row_maps)


finest_tier = lax.Precision.HIGHEST


def pick_rows(block, rows_list):
    return block[rows_list]


def place_rows(block, left_part, right_part, left_vals, right_vals):
    return block.at[left_part].add(left_vals).at[right_part].add(right_vals)


def assemble_dual(deformation_vector, left_neighbour_rows, right_neighbour_rows):
    to_right = jax.vmap(pick_rows)(deformation_vector, right_neighbour_rows)
    to_left = jax.vmap(pick_rows)(deformation_vector, left_neighbour_rows)
    blank = jnp.zeros_like(to_right[:1])
    from_left = jnp.concatenate([blank, to_right[:-1]], axis=0)
    from_right = jnp.concatenate([to_left[1:], blank], axis=0)
    return jax.vmap(place_rows)(deformation_vector, left_neighbour_rows, right_neighbour_rows, from_left, from_right)


def chain_weights(left_neighbour_rows, right_neighbour_rows):
    places = jnp.arange(SUBS)

    def weigh(place, left_part, right_part):
        weight = jnp.ones((M,), jnp.float32)
        weight = weight.at[left_part].set(jnp.where(place > 0, 0.5, 1.0).astype(jnp.float32))
        weight = weight.at[right_part].set(jnp.where(place < SUBS - 1, 0.5, 1.0).astype(jnp.float32))
        return weight

    return jax.vmap(weigh)(places, left_neighbour_rows, right_neighbour_rows)[:, :, None]


def inner_product(first, second, interface_weights):
    return jnp.sum(interface_weights * first * second, axis=(0, 1))


def project(deformation_vector, kernel_coefficients, coarse_rows, left_neighbour_rows, right_neighbour_rows):
    kernel_basis_matrix = jnp.einsum('tgh,thz->tgz', kernel_coefficients, deformation_vector, precision=finest_tier)
    load_amounts = jnp.dot(coarse_rows, kernel_basis_matrix.reshape(COARSE, R), precision=finest_tier).reshape(SUBS, MODES, R)
    return_back = jnp.einsum('tyh,tye->the', kernel_coefficients, load_amounts, precision=finest_tier)
    return deformation_vector - assemble_dual(return_back, left_neighbour_rows, right_neighbour_rows)


def reference(dual_ops, boundary_solve_blocks, rigid_images, coarse_rows, gap_raw, row_maps):
    dual_operator = dual_ops.reshape(SUBS, M, M)
    dirichlet_preconditioner = boundary_solve_blocks.reshape(SUBS, M, M)
    kernel_coefficients = rigid_images.reshape(SUBS, MODES, M)
    left_neighbour_rows = row_maps[:, 0, :]
    right_neighbour_rows = row_maps[:, 1, :]
    interface_weights = chain_weights(left_neighbour_rows, right_neighbour_rows)
    residual = assemble_dual(gap_raw.reshape(SUBS, M, R), left_neighbour_rows, right_neighbour_rows)
    multipliers = jnp.zeros((SUBS, M, R), jnp.float32)
    norm_list = []
    search_direction = multipliers
    previous_norm = jnp.ones((R,), jnp.float32)
    for iteration in range(ITERS):
        norm_list.append(inner_product(residual, residual, interface_weights))
        projected_residual = project(residual, kernel_coefficients, coarse_rows, left_neighbour_rows, right_neighbour_rows)
        local_contributions = jnp.einsum('hlf,hfz->hlz', dirichlet_preconditioner, interface_weights * projected_residual, precision=finest_tier)
        smoothed = interface_weights * assemble_dual(local_contributions, left_neighbour_rows, right_neighbour_rows)
        update = project(smoothed, kernel_coefficients, coarse_rows, left_neighbour_rows, right_neighbour_rows)
        precond_norm = inner_product(projected_residual, smoothed, interface_weights)
        if iteration == 0:
            search_direction = update
        else:
            search_direction = update + (precond_norm / previous_norm) * search_direction
        rigid_image = assemble_dual(jnp.einsum('hlf,hfz->hlz', dual_operator, search_direction, precision=finest_tier), left_neighbour_rows, right_neighbour_rows)
        step_size = precond_norm / inner_product(search_direction, rigid_image, interface_weights)
        multipliers = multipliers + step_size * search_direction
        residual = residual - step_size * rigid_image
        previous_norm = precond_norm
    return multipliers.reshape(SUBS * M, R), residual.reshape(SUBS * M, R), jnp.stack(norm_list)
```

```python
import jax
import jax.numpy as jnp
from jax import lax
from jax.sharding import Mesh
from jax.sharding import PartitionSpec as P

ITERS = 2
CLUSTER_SUB = ("cluster", "sub_0", "sub_1", "sub_2")
OUTER = ("cluster", "sub_0")
INNER = ("sub_1", "sub_2")
TILE = 8

FULL = lax.Precision.HIGHEST
THREE = lax.Precision.HIGH


def passed_along(value, axis, steps):
    count = lax.axis_size(axis)
    first, last = max(0, -steps), min(count, count - steps)
    return lax.ppermute(value, axis, [(s, s + steps) for s in range(first, last)])


def dot(a, b, precision=FULL):
    return jnp.dot(a, b, precision=precision, preferred_element_type=jnp.float32)


def tdot(a, b, precision=FULL):
    return lax.dot_general(
        a, b, (((0,), (0,)), ((), ())), precision=precision, preferred_element_type=jnp.float32
    )


def swap(blocks, axis):
    return lax.all_to_all(blocks, axis, split_axis=0, concat_axis=0, tiled=True)


def shards(dual_ops, boundary_solve_blocks, rigid_images, coarse_rows, gap_raw, row_maps):
    modes, local_rows = rigid_images.shape
    cases = gap_raw.shape[1]
    count = lax.axis_size(CLUSTER_SUB)
    outer, inner = lax.axis_size(OUTER), lax.axis_size(INNER)
    place = lax.axis_index(CLUSTER_SUB)
    left, right = row_maps[0, 0], row_maps[0, 1]
    shared = left.shape[0]

    block = swap(coarse_rows.reshape(modes, outer, inner * modes).transpose(1, 0, 2), OUTER)
    block = jnp.pad(
        block.reshape(outer, modes, inner, modes),
        ((0, 0), (0, TILE - modes), (0, 0), (0, TILE - modes)),
    )
    tile_row = lax.broadcasted_iota(jnp.int32, (1, TILE, 1, TILE), 1)
    tile_col = lax.broadcasted_iota(jnp.int32, (1, TILE, 1, TILE), 3)
    sums = ((tile_row == tile_col) & (tile_row >= modes)).astype(jnp.float32)
    block = (block + sums).reshape(outer * TILE, inner * TILE)

    def coarse(pack):
        near = swap(jnp.broadcast_to(pack, (inner, TILE, cases)), INNER)
        partial = dot(block, near.reshape(inner * TILE, cases))
        return jnp.sum(swap(partial.reshape(outer, TILE, cases), OUTER), axis=0)

    def extended(amounts):
        return jnp.concatenate(
            [
                amounts,
                passed_along(amounts, CLUSTER_SUB, 1),
                passed_along(amounts, CLUSTER_SUB, -1),
            ],
            axis=0,
        )

    picks = jnp.concatenate([left, right])
    selector = (picks[:, None] == lax.broadcasted_iota(jnp.int32, (2 * shared, local_rows), 1)).astype(
        jnp.float32
    )
    is_left = jnp.sum(selector[:shared], axis=0)
    is_right = jnp.sum(selector[shared:], axis=0)
    halves = jnp.where(place > 0, 0.5, 0.0) * is_left + jnp.where(place < count - 1, 0.5, 0.0) * is_right
    weights = (1.0 - halves)[:, None]

    def exchanged(to_right, to_left):
        return (
            passed_along(to_right, CLUSTER_SUB, 1),
            passed_along(to_left, CLUSTER_SUB, -1),
        )

    def scattered(y, from_left, from_right):
        return y.at[left].add(from_left).at[right].add(from_right)

    def assemble(y):
        return scattered(y, *exchanged(y[right], y[left]))

    rigid_shared = lax.dot_general(
        rigid_images, selector, (((1,), (1,)), ((), ())), precision=FULL,
        preferred_element_type=jnp.float32,
    )
    near_left, near_right = exchanged(rigid_shared[:, shared:], rigid_shared[:, :shared])
    spare = jnp.zeros((TILE - modes, local_rows), jnp.float32)
    rigid_extended = jnp.concatenate(
        [
            rigid_images,
            spare,
            dot(near_left, selector[:shared]),
            spare,
            dot(near_right, selector[shared:]),
            spare,
        ],
        axis=0,
    )

    def packed(modes_part, first, second):
        return jnp.concatenate([modes_part, first[None], second[None]], axis=0)

    zero = jnp.zeros((cases,), jnp.float32)

    def precondition(residual, amounts):
        projected = residual - tdot(rigid_extended, amounts)
        weighted = weights * projected
        solved = dot(boundary_solve_blocks, weighted, THREE)
        part = jnp.sum(weighted * solved, axis=0)
        return weights * assemble(solved), part

    residual = assemble(gap_raw)
    norm_part = jnp.sum(weights * residual * residual, axis=0)
    total = coarse(packed(dot(rigid_images, residual), norm_part, zero))
    norm_first = total[modes]
    amounts = extended(total)

    smoothed, part = precondition(residual, amounts)
    total = coarse(packed(dot(rigid_images, smoothed), part, zero))
    precond_norm = total[modes]
    direction = smoothed - tdot(rigid_extended, extended(total))
    image = dot(dual_ops, direction, THREE)
    part = jnp.sum(direction * image, axis=0)
    image = assemble(image)
    total = coarse(packed(dot(rigid_images, image), part, zero))
    step = precond_norm / total[modes]
    multipliers = step * direction
    residual = residual - step * image
    norm_part = jnp.sum(weights * residual * residual, axis=0)
    amounts = amounts - step * extended(total)

    smoothed, part = precondition(residual, amounts)
    total = coarse(packed(dot(rigid_images, smoothed), part, norm_part))
    norm_second = total[modes + 1]
    update = smoothed - tdot(rigid_extended, extended(total))
    direction = update + total[modes] / precond_norm * direction
    precond_norm = total[modes]
    image = dot(dual_ops, direction, THREE)
    part = jnp.sum(direction * image, axis=0)
    bending = jnp.sum(swap(jnp.broadcast_to(part, (count, 1, cases)), CLUSTER_SUB), axis=0)[0]
    image = assemble(image)
    step = precond_norm / bending
    multipliers = multipliers + step * direction
    residual = residual - step * image
    return (multipliers, residual, jnp.stack([norm_first, norm_second]))


def solution(mesh):
    devices = mesh.devices
    x, sub = devices.shape
    sizes = (x, 4, sub // 8, 2)
    split = Mesh(devices.reshape(sizes), CLUSTER_SUB)
    in_specs = (P(CLUSTER_SUB, None),) * 5 + (P(CLUSTER_SUB, None, None),)
    out_specs = (P(CLUSTER_SUB, None), P(CLUSTER_SUB, None), P())
    return jax.shard_map(
        shards, mesh=split, in_specs=in_specs, out_specs=out_specs, check_vma=False
    )
```

```python
import jax
import jax.numpy as jnp
from jax import lax
from jax.sharding import Mesh
from jax.sharding import PartitionSpec as P

ITERS = 2
CLUSTER_SUB = ("cluster", "sub_0", "sub_1", "sub_2")
OUTER = ("cluster", "sub_0")
INNER = ("sub_1", "sub_2")
TILE = 8

FULL = lax.Precision.HIGHEST
THREE = lax.Precision.HIGH


def matched(value, pairs):
    return lax.ppermute(value, CLUSTER_SUB, pairs)


def matchings(count):
    near = [(i, i ^ 1) for i in range(count)]
    far = [(i, i if i in (0, count - 1) else ((i + 1) ^ 1) - 1) for i in range(count)]
    return near, far


def dot(a, b, precision=FULL):
    return jnp.dot(a, b, precision=precision, preferred_element_type=jnp.float32)


def tdot(a, b, precision=FULL):
    return lax.dot_general(
        a, b, (((0,), (0,)), ((), ())), precision=precision, preferred_element_type=jnp.float32
    )


def swap(blocks, axis):
    return lax.all_to_all(blocks, axis, split_axis=0, concat_axis=0, tiled=True)


def shards(dual_ops, boundary_solve_blocks, rigid_images, coarse_rows, gap_raw, row_maps):
    modes, local_rows = rigid_images.shape
    cases = gap_raw.shape[1]
    count = lax.axis_size(CLUSTER_SUB)
    outer, inner = lax.axis_size(OUTER), lax.axis_size(INNER)
    place = lax.axis_index(CLUSTER_SUB)
    even = place % 2 == 0
    inside = jnp.where((place > 0) & (place < count - 1), 1.0, 0.0).astype(jnp.float32)
    mate = jnp.where(even, row_maps[0, 1], row_maps[0, 0])
    far = jnp.where(even, row_maps[0, 0], row_maps[0, 1])
    shared = mate.shape[0]
    mate_pairs, far_pairs = matchings(count)

    def exchanged(to_mate, to_far):
        from_far = matched(to_far, far_pairs)
        from_mate = matched(to_mate, mate_pairs)
        return from_mate, inside * from_far

    def assemble(y):
        from_mate, from_far = exchanged(y[mate], y[far])
        return y.at[mate].add(from_mate).at[far].add(from_far)

    residual = assemble(gap_raw)

    picks = jnp.concatenate([mate, far])
    selector = (picks[:, None] == lax.broadcasted_iota(jnp.int32, (2 * shared, local_rows), 1)).astype(
        jnp.float32
    )
    on_mate = jnp.sum(selector[:shared], axis=0)
    on_far = jnp.sum(selector[shared:], axis=0)
    weights = (1.0 - 0.5 * on_mate - 0.5 * inside * on_far)[:, None]

    rigid_shared = lax.dot_general(
        rigid_images, selector, (((1,), (1,)), ((), ())), precision=FULL,
        preferred_element_type=jnp.float32,
    )
    from_mate, from_far = exchanged(
        jnp.concatenate([coarse_rows, rigid_shared[:, :shared]], axis=1),
        jnp.concatenate([coarse_rows, rigid_shared[:, shared:]], axis=1),
    )
    order = coarse_rows.shape[1]
    spare = jnp.zeros((TILE - modes, local_rows), jnp.float32)
    rigid_extended = jnp.concatenate(
        [
            rigid_images,
            spare,
            dot(from_mate[:, order:], selector[:shared]),
            spare,
            dot(from_far[:, order:], selector[shared:]),
            spare,
        ],
        axis=0,
    )

    tall = jnp.concatenate([coarse_rows, from_mate[:, :order], from_far[:, :order]], axis=0)
    block = swap(tall.reshape(3 * modes, outer, inner * modes).transpose(1, 0, 2), OUTER)
    block = jnp.pad(
        block.reshape(outer, 3, modes, inner, modes),
        ((0, 0), (0, 0), (0, TILE - modes), (0, 0), (0, TILE - modes)),
    )
    shape = (1, 3, TILE, 1, TILE)
    part_of = lax.broadcasted_iota(jnp.int32, shape, 1)
    tile_row = lax.broadcasted_iota(jnp.int32, shape, 2)
    tile_col = lax.broadcasted_iota(jnp.int32, shape, 4)
    sums = ((part_of == 0) & (tile_row == tile_col) & (tile_row >= modes)).astype(jnp.float32)
    block = (block + sums).reshape(outer * 3 * TILE, inner * TILE)

    def coarse(pack):
        near = swap(jnp.broadcast_to(pack, (inner, TILE, cases)), INNER)
        partial = dot(block, near.reshape(inner * TILE, cases))
        return jnp.sum(swap(partial.reshape(outer, 3 * TILE, cases), OUTER), axis=0)

    def packed(modes_part, first, second):
        return jnp.concatenate([modes_part, first[None], second[None]], axis=0)

    zero = jnp.zeros((cases,), jnp.float32)

    def precondition(residual, amounts):
        projected = residual - tdot(rigid_extended, amounts)
        weighted = weights * projected
        solved = dot(boundary_solve_blocks, weighted, THREE)
        part = jnp.sum(weighted * solved, axis=0)
        return weights * assemble(solved), part

    norm_part = jnp.sum(weights * residual * residual, axis=0)
    total = coarse(packed(dot(rigid_images, residual), norm_part, zero))
    norm_first = total[modes]
    amounts = total

    smoothed, part = precondition(residual, amounts)
    total = coarse(packed(dot(rigid_images, smoothed), part, zero))
    precond_norm = total[modes]
    direction = smoothed - tdot(rigid_extended, total)
    image = dot(dual_ops, direction, THREE)
    part = jnp.sum(direction * image, axis=0)
    image = assemble(image)
    total = coarse(packed(dot(rigid_images, image), part, zero))
    step = precond_norm / total[modes]
    multipliers = step * direction
    residual = residual - step * image
    norm_part = jnp.sum(weights * residual * residual, axis=0)
    amounts = amounts - step * total

    smoothed, part = precondition(residual, amounts)
    total = coarse(packed(dot(rigid_images, smoothed), part, norm_part))
    norm_second = total[modes + 1]
    update = smoothed - tdot(rigid_extended, total)
    direction = update + total[modes] / precond_norm * direction
    precond_norm = total[modes]
    image = dot(dual_ops, direction, THREE)
    part = jnp.sum(direction * image, axis=0)
    bending = jnp.sum(swap(jnp.broadcast_to(part, (count, 1, cases)), CLUSTER_SUB), axis=0)[0]
    image = assemble(image)
    step = precond_norm / bending
    multipliers = multipliers + step * direction
    residual = residual - step * image
    return (multipliers, residual, jnp.stack([norm_first, norm_second]))


def solution(mesh):
    devices = mesh.devices
    x, sub = devices.shape
    sizes = (x, 4, sub // 8, 2)
    split = Mesh(devices.reshape(sizes), CLUSTER_SUB)
    in_specs = (P(CLUSTER_SUB, None),) * 5 + (P(CLUSTER_SUB, None, None),)
    out_specs = (P(CLUSTER_SUB, None), P(CLUSTER_SUB, None), P())
    return jax.shard_map(
        shards, mesh=split, in_specs=in_specs, out_specs=out_specs, check_vma=False
    )
```

```python
import functools

import jax
import jax.numpy as jnp
from jax import lax
from jax.experimental import pallas as pl
from jax.experimental.pallas import tpu as pltpu
from jax.sharding import Mesh
from jax.sharding import PartitionSpec as P

CLUSTER_SUB = ("cluster", "sub_0", "sub_1", "sub_2")
OUTER = ("cluster", "sub_0")
INNER = ("sub_1", "sub_2")
TILE = 8
ROWS = 256
VMEM_LIMIT = 24 * 1024 * 1024

FULL = lax.Precision.HIGHEST
F32 = jnp.float32
BF16 = jnp.bfloat16


def dot(a, b, precision=FULL):
    return jnp.dot(a, b, precision=precision, preferred_element_type=F32)


def fast(a, b):
    return jnp.dot(a, b, preferred_element_type=F32)


def halves(value):
    high = value.astype(BF16)
    return high, (value - high.astype(F32)).astype(BF16)


def rounded_halves(value):
    high = lax.reduce_precision(value, exponent_bits=8, mantissa_bits=7)
    return high.astype(BF16), (value - high).astype(BF16)


def swap(blocks, axis):
    return lax.all_to_all(blocks, axis, split_axis=0, concat_axis=0, tiled=True)


def matched(value, pairs):
    return lax.ppermute(value, CLUSTER_SUB, pairs)


def matchings(count):
    near = [(i, i ^ 1) for i in range(count)]
    far = [(i, i if i in (0, count - 1) else ((i + 1) ^ 1) - 1) for i in range(count)]
    return near, far


def call(body, out_shapes, scratch, flops, moved):
    def run(*operands):
        return pl.pallas_call(
            body,
            out_shape=[jax.ShapeDtypeStruct(s, F32) for s in out_shapes],
            in_specs=[pl.BlockSpec(memory_space=pltpu.VMEM)] * len(operands),
            out_specs=[pl.BlockSpec(memory_space=pltpu.VMEM)] * len(out_shapes),
            scratch_shapes=scratch,
            compiler_params=pltpu.CompilerParams(vmem_limit_bytes=VMEM_LIMIT),
            cost_estimate=pl.CostEstimate(flops=flops, bytes_accessed=moved, transcendentals=0),
        )(*operands)

    return run


def summed(near_ref):
    total = near_ref[0]
    for member in range(1, near_ref.shape[0]):
        total = total + near_ref[member]
    return total


def stacked(amounts):
    spare = jnp.zeros((TILE, amounts.shape[1]), F32)
    high, low = halves(jnp.concatenate([amounts, spare], axis=0))
    return jnp.concatenate([high, low, high], axis=0)


def blocks_of(rows, body, start):
    return lax.fori_loop(0, rows // ROWS, lambda i, c: body(pl.ds(pl.multiple_of(i * ROWS, ROWS), ROWS), i, c), start)


def multiply(m_ref, s_ref, x_ref, high_ref, low_ref, out_ref, mate_ref, far_ref, part_ref):
    rows, cases = out_ref.shape
    shared = mate_ref.shape[0]
    xh, xl = high_ref[...], low_ref[...]

    def step(at, i, carry):
        part, sent = carry
        mh, ml = halves(m_ref[at, :])
        out = fast(mh, xh) + fast(mh, xl) + fast(ml, xh)
        out_ref[at, :] = out
        part = part + jnp.sum(x_ref[at, :] * out, axis=0, keepdims=True)
        uh, ul = halves(out)
        pick = s_ref[i]
        return part, sent + fast(pick, uh) + fast(pick, ul)

    start = (jnp.zeros((1, cases), F32), jnp.zeros((2 * shared, cases), F32))
    part, sent = blocks_of(rows, step, start)
    part_ref[...] = part
    mate_ref[...] = sent[:shared]
    far_ref[...] = sent[shared:]


def keep(at, x, x_ref, high_ref, low_ref):
    x_ref[at, :] = x
    high_ref[at, :], low_ref[at, :] = halves(x)


def precondition_first(near_ref, r_ref, w_ref, rt_ref, m_ref, s_ref,
                       out_ref, mate_ref, far_ref, part_ref, total_ref, x_ref, high_ref, low_ref):
    total = summed(near_ref)
    total_ref[...] = total
    amounts = stacked(total)

    def step(at, i, carry):
        keep(at, w_ref[at, :] * (r_ref[at, :] - fast(rt_ref[at, :], amounts)), x_ref, high_ref, low_ref)
        return carry

    blocks_of(r_ref.shape[0], step, 0)
    multiply(m_ref, s_ref, x_ref, high_ref, low_ref, out_ref, mate_ref, far_ref, part_ref)


def direct_first(near_ref, v_ref, rt_ref, m_ref, s_ref,
                 out_ref, mate_ref, far_ref, part_ref, total_ref, x_ref, high_ref, low_ref):
    total = summed(near_ref)
    total_ref[...] = total
    amounts = stacked(total)

    def step(at, i, carry):
        keep(at, v_ref[at, :] - fast(rt_ref[at, :], amounts), x_ref, high_ref, low_ref)
        return carry

    blocks_of(v_ref.shape[0], step, 0)
    multiply(m_ref, s_ref, x_ref, high_ref, low_ref, out_ref, mate_ref, far_ref, part_ref)


def precondition_next(modes, near_ref, before_ref, norm_ref, r_ref, image_ref, w_ref, rt_ref, m_ref, s_ref,
                      out_ref, mate_ref, far_ref, part_ref, size_ref, r_out_ref, step_ref, x_ref, high_ref, low_ref):
    total = summed(near_ref)
    length = norm_ref[modes:modes + 1, :] / total[modes:modes + 1]
    step_ref[...] = length
    amounts = stacked(before_ref[...] - length * total)

    def step(at, i, size):
        residual = r_ref[at, :] - length * image_ref[at, :]
        r_out_ref[at, :] = residual
        weighted = w_ref[at, :] * residual
        keep(at, w_ref[at, :] * (residual - fast(rt_ref[at, :], amounts)), x_ref, high_ref, low_ref)
        return size + jnp.sum(weighted * residual, axis=0, keepdims=True)

    size_ref[...] = blocks_of(r_ref.shape[0], step, jnp.zeros((1, r_ref.shape[1]), F32))
    multiply(m_ref, s_ref, x_ref, high_ref, low_ref, out_ref, mate_ref, far_ref, part_ref)


def direct_next(modes, near_ref, norm_ref, v_ref, d_ref, rt_ref, m_ref, s_ref,
                out_ref, mate_ref, far_ref, part_ref, total_ref, x_ref, high_ref, low_ref):
    total = summed(near_ref)
    total_ref[...] = total
    ratio = total[modes:modes + 1] / norm_ref[modes:modes + 1, :]
    amounts = stacked(total)

    def step(at, i, carry):
        update = v_ref[at, :] - fast(rt_ref[at, :], amounts)
        keep(at, update + ratio * d_ref[at, :], x_ref, high_ref, low_ref)
        return carry

    blocks_of(v_ref.shape[0], step, 0)
    multiply(m_ref, s_ref, x_ref, high_ref, low_ref, out_ref, mate_ref, far_ref, part_ref)


def received(mate_ref, far_ref):
    return halves(jnp.concatenate([mate_ref[...], far_ref[...]], axis=0))


def pack_out(modes, pack_ref, sums, low_sums, first, second):
    part = sums[:TILE] + sums[TILE:] + low_sums[:TILE]
    row = lax.broadcasted_iota(jnp.int32, part.shape, 0)
    part = jnp.where(row == modes, first, jnp.where(row == modes + 1, second, part))
    for member in range(pack_ref.shape[0]):
        pack_ref[member] = part


def gather_modes(rigid_ref, value, i, sums, low_sums):
    zh, zl = halves(value)
    rigid = rigid_ref[i]
    return sums + fast(rigid, zh), low_sums + fast(rigid, zl)


def start_body(modes, y_ref, mate_ref, far_ref, st_ref, w_ref, rigid_ref, out_ref, pack_ref):
    rh, rl = received(mate_ref, far_ref)
    cases = y_ref.shape[1]

    def step(at, i, carry):
        size, sums, low_sums = carry
        place = st_ref[at, :]
        value = y_ref[at, :] + (fast(place, rh) + fast(place, rl))
        out_ref[at, :] = value
        size = size + jnp.sum(w_ref[at, :] * value * value, axis=0, keepdims=True)
        return (size, *gather_modes(rigid_ref, value, i, sums, low_sums))

    zeros = jnp.zeros((2 * TILE, cases), F32)
    size, sums, low_sums = blocks_of(y_ref.shape[0], step, (jnp.zeros((1, cases), F32), zeros, zeros))
    pack_out(modes, pack_ref, sums, low_sums, size, jnp.zeros_like(size))


def assemble_body(modes, weighted, sized, *refs):
    y_ref, mate_ref, far_ref, st_ref, rigid_ref, part_ref = refs[:6]
    w_ref = refs[6] if weighted else None
    size_ref = refs[6 + weighted] if sized else None
    out_ref, pack_ref = refs[6 + weighted + sized:]
    rh, rl = received(mate_ref, far_ref)

    def step(at, i, carry):
        place = st_ref[at, :]
        value = y_ref[at, :] + (fast(place, rh) + fast(place, rl))
        if weighted:
            value = w_ref[at, :] * value
        out_ref[at, :] = value
        return gather_modes(rigid_ref, value, i, *carry)

    zeros = jnp.zeros((2 * TILE, y_ref.shape[1]), F32)
    sums, low_sums = blocks_of(y_ref.shape[0], step, (zeros, zeros))
    part = part_ref[...]
    pack_out(modes, pack_ref, sums, low_sums, part, size_ref[...] if sized else jnp.zeros_like(part))


def block_body(block_ref, near_ref, out_ref):
    members, tile, cases = near_ref.shape
    high, low = halves(near_ref[...].reshape(members * tile, cases))
    out = fast(block_ref[...], jnp.concatenate([high, low, high], axis=0))
    out_ref[...] = out.reshape(out_ref.shape)


def finish_body(q_ref, mate_ref, far_ref, st_ref, r_ref, first_ref, second_ref, step_first_ref, step_ref,
                multipliers_ref, residual_ref):
    rh, rl = received(mate_ref, far_ref)
    first, second = step_first_ref[...], step_ref[...]

    def step(at, i, carry):
        place = st_ref[at, :]
        image = q_ref[at, :] + (fast(place, rh) + fast(place, rl))
        multipliers_ref[at, :] = first * first_ref[at, :] + second * second_ref[at, :]
        residual_ref[at, :] = r_ref[at, :] - second * image
        return carry

    blocks_of(q_ref.shape[0], step, 0)


def shards(dual_ops, boundary_solve_blocks, rigid_images, coarse_rows, gap_raw, row_maps):
    modes, local_rows = rigid_images.shape
    cases = gap_raw.shape[1]
    count = lax.axis_size(CLUSTER_SUB)
    outer, inner = lax.axis_size(OUTER), lax.axis_size(INNER)
    place = lax.axis_index(CLUSTER_SUB)
    even = place % 2 == 0
    inside = jnp.where((place > 0) & (place < count - 1), 1.0, 0.0).astype(F32)
    mate = jnp.where(even, row_maps[0, 1], row_maps[0, 0])
    far = jnp.where(even, row_maps[0, 0], row_maps[0, 1])
    shared = mate.shape[0]
    mate_pairs, far_pairs = matchings(count)

    def exchanged(to_mate, to_far):
        from_far = matched(to_far, far_pairs)
        from_mate = matched(to_mate, mate_pairs)
        return from_mate, from_far

    gap_near = exchanged(gap_raw[mate], gap_raw[far])

    picks = jnp.concatenate([mate, far])
    live = jnp.concatenate([jnp.ones((shared,), F32), jnp.full((shared,), inside)])
    one_hot = jnp.where(
        picks[:, None] == lax.broadcasted_iota(jnp.int32, (2 * shared, local_rows), 1), live[:, None], 0.0
    )
    selector = one_hot.astype(BF16).reshape(2 * shared, local_rows // ROWS, ROWS).transpose(1, 0, 2)
    placer = jnp.where(
        picks[None, :] == lax.broadcasted_iota(jnp.int32, (local_rows, 2 * shared), 0), live[None, :], 0.0
    )
    weights = jnp.broadcast_to(1.0 - 0.5 * jnp.sum(placer, axis=1, keepdims=True), (local_rows, cases))
    placer = placer.astype(BF16)

    rigid_shared = lax.dot_general(
        rigid_images, one_hot, (((1,), (1,)), ((), ())), precision=FULL, preferred_element_type=F32
    )
    from_mate, from_far = exchanged(
        jnp.concatenate([coarse_rows, rigid_shared[:, :shared]], axis=1),
        jnp.concatenate([coarse_rows, rigid_shared[:, shared:]], axis=1),
    )
    order = coarse_rows.shape[1]

    def across(near, hot):
        return lax.dot_general(
            hot, near, (((0,), (1,)), ((), ())), precision=FULL, preferred_element_type=F32
        )

    gap = jnp.zeros((local_rows, TILE - modes), F32)
    rigid_tall = jnp.concatenate(
        [
            rigid_images.T,
            gap,
            across(from_mate[:, order:], one_hot[:shared]),
            gap,
            across(from_far[:, order:], one_hot[shared:]),
            gap,
            jnp.zeros((local_rows, TILE), F32),
        ],
        axis=1,
    )
    tall_high, tall_low = rounded_halves(rigid_tall)
    rigid_tall = jnp.concatenate([tall_high, tall_high, tall_low], axis=1)
    wide_high, wide_low = rounded_halves(jnp.pad(rigid_images, ((0, TILE - modes), (0, 0))))
    rigid_wide = jnp.concatenate([wide_high, wide_low], axis=0)
    rigid_wide = rigid_wide.reshape(2 * TILE, local_rows // ROWS, ROWS).transpose(1, 0, 2)

    rows_here = jnp.concatenate([coarse_rows, from_mate[:, :order], from_far[:, :order]], axis=0)
    block = swap(rows_here.reshape(3 * modes, outer, inner * modes).transpose(1, 0, 2), OUTER)
    block = jnp.pad(
        block.reshape(outer, 3, modes, inner, modes),
        ((0, 0), (0, 0), (0, TILE - modes), (0, 0), (0, TILE - modes)),
    )
    shape = (1, 3, TILE, 1, TILE)
    part_of = lax.broadcasted_iota(jnp.int32, shape, 1)
    tile_row = lax.broadcasted_iota(jnp.int32, shape, 2)
    tile_col = lax.broadcasted_iota(jnp.int32, shape, 4)
    sums = ((part_of == 0) & (tile_row == tile_col) & (tile_row >= modes)).astype(F32)
    block_high, block_low = rounded_halves((block + sums).reshape(outer * 3 * TILE, inner * TILE))
    block = jnp.concatenate([block_high, block_high, block_low], axis=1)

    field = (local_rows, cases)
    edge = (shared, cases)
    row = (1, cases)
    rows_out = (3 * TILE, cases)
    pack_shape = (inner, TILE, cases)
    scratch = [pltpu.VMEM(field, F32), pltpu.VMEM(field, BF16), pltpu.VMEM(field, BF16)]
    own = scratch[1:]
    big = 6 * local_rows * local_rows * cases
    light = 4 * local_rows * cases * 2 * shared
    moved = 4 * local_rows * (local_rows + 3 * cases)

    def coarse(pack):
        near = swap(pack, INNER)
        [rows] = call(block_body, [(outer, 3 * TILE, cases)], [], 6 * block.shape[0] * block.shape[1] * cases,
                      4 * outer * 4 * TILE * cases)(block, near)
        return swap(rows, OUTER)

    def assemble(weighted, sized, *operands):
        body = functools.partial(assemble_body, modes, weighted, sized)
        return call(body, [field, pack_shape], [], light, 12 * local_rows * cases)(*operands)

    residual, pack = call(functools.partial(start_body, modes), [field, pack_shape], [], light, 12 * local_rows * cases)(
        gap_raw, *gap_near, placer, weights, rigid_wide
    )
    near = coarse(pack)
    out, to_mate, to_far, part, amounts = call(
        precondition_first, [field, edge, edge, row, rows_out], scratch, big, moved
    )(near, residual, weights, rigid_tall, boundary_solve_blocks, selector)
    norm_first = amounts[modes]
    smoothed, pack = assemble(True, False, out, *exchanged(to_mate, to_far), placer, rigid_wide, part, weights)
    near = coarse(pack)
    out, to_mate, to_far, part, total, direction_first = call(
        direct_first, [field, edge, edge, row, rows_out, field], own, big, moved
    )(near, smoothed, rigid_tall, dual_ops, selector)
    image, pack = assemble(False, False, out, *exchanged(to_mate, to_far), placer, rigid_wide, part)
    near = coarse(pack)
    out, to_mate, to_far, part, size, residual, step_first = call(
        functools.partial(precondition_next, modes), [field, edge, edge, row, row, field, row], scratch, big, moved
    )(near, amounts, total, residual, image, weights, rigid_tall, boundary_solve_blocks, selector)
    smoothed, pack = assemble(True, True, out, *exchanged(to_mate, to_far), placer, rigid_wide, part, weights, size)
    near = coarse(pack)
    out, to_mate, to_far, part, last, direction = call(
        functools.partial(direct_next, modes), [field, edge, edge, row, rows_out, field], own, big, moved
    )(near, total, smoothed, direction_first, rigid_tall, dual_ops, selector)
    norm_second = last[modes + 1]
    from_mate, from_far = exchanged(to_mate, to_far)
    bending = jnp.sum(swap(jnp.broadcast_to(part, (count, 1, cases)), CLUSTER_SUB), axis=0)
    step = last[modes:modes + 1] / bending
    multipliers, residual = call(finish_body, [field, field], [], light, 24 * local_rows * cases)(
        out, from_mate, from_far, placer, residual, direction_first, direction, step_first, step
    )
    return (multipliers, residual, jnp.stack([norm_first, norm_second]))


def solution(mesh):
    devices = mesh.devices
    x, sub = devices.shape
    split = Mesh(devices.reshape(x, 4, sub // 8, 2), CLUSTER_SUB)
    in_specs = (P(CLUSTER_SUB, None),) * 5 + (P(CLUSTER_SUB, None, None),)
    out_specs = (P(CLUSTER_SUB, None), P(CLUSTER_SUB, None), P())
    return jax.shard_map(
        shards, mesh=split, in_specs=in_specs, out_specs=out_specs, check_vma=False
    )
```

```python
import functools

import jax
import jax.numpy as jnp
from jax import lax
from jax.experimental import pallas as pl
from jax.experimental.pallas import tpu as pltpu
from jax.sharding import Mesh
from jax.sharding import PartitionSpec as P

CLUSTER_SUB = ("cluster", "sub_0", "sub_1", "sub_2")
OUTER = ("cluster", "sub_0")
INNER = ("sub_1", "sub_2")
TILE = 8
ROWS = 256
VMEM_LIMIT = 24 * 1024 * 1024

F32 = jnp.float32
BF16 = jnp.bfloat16


def fast(a, b):
    return jnp.dot(a, b, preferred_element_type=F32)


def halves(value):
    high = value.astype(BF16)
    return high, (value - high.astype(F32)).astype(BF16)


def swap(blocks, axis):
    return lax.all_to_all(blocks, axis, split_axis=0, concat_axis=0, tiled=True)


def matched(value, pairs):
    return lax.ppermute(value, CLUSTER_SUB, pairs)


def matchings(count):
    near = [(i, i ^ 1) for i in range(count)]
    far = [(i, i if i in (0, count - 1) else ((i + 1) ^ 1) - 1) for i in range(count)]
    return near, far


def call(body, out_shapes, scratch, flops, moved):
    def run(*operands):
        return pl.pallas_call(
            body,
            out_shape=[s if hasattr(s, "dtype") else jax.ShapeDtypeStruct(s, F32) for s in out_shapes],
            in_specs=[pl.BlockSpec(memory_space=pltpu.VMEM)] * len(operands),
            out_specs=[pl.BlockSpec(memory_space=pltpu.VMEM)] * len(out_shapes),
            scratch_shapes=scratch,
            compiler_params=pltpu.CompilerParams(vmem_limit_bytes=VMEM_LIMIT),
            cost_estimate=pl.CostEstimate(flops=flops, bytes_accessed=moved, transcendentals=0),
        )(*operands)

    return run


def summed(near_ref):
    total = near_ref[0]
    for member in range(1, near_ref.shape[0]):
        total = total + near_ref[member]
    return total


def stacked(amounts):
    spare = jnp.zeros((TILE, amounts.shape[1]), F32)
    high, low = halves(jnp.concatenate([amounts, spare], axis=0))
    return jnp.concatenate([high, low, high, jnp.zeros_like(high)], axis=0)


def blocks_of(rows, body, start):
    return lax.fori_loop(0, rows // ROWS, lambda i, c: body(pl.ds(pl.multiple_of(i * ROWS, ROWS), ROWS), i, c), start)


def multiply(m_ref, s_ref, x_ref, high_ref, low_ref, out_ref, mate_ref, far_ref, part_ref):
    rows, cases = out_ref.shape
    shared = mate_ref.shape[0]
    xh, xl = high_ref[...], low_ref[...]

    def step(at, i, carry):
        part, sent = carry
        mh, ml = halves(m_ref[at, :])
        out = fast(mh, xh) + fast(mh, xl) + fast(ml, xh)
        out_ref[at, :] = out
        part = part + jnp.sum(x_ref[at, :] * out, axis=0, keepdims=True)
        uh, ul = halves(out)
        pick = s_ref[i]
        return part, sent + fast(pick, uh) + fast(pick, ul)

    start = (jnp.zeros((1, cases), F32), jnp.zeros((2 * shared, cases), F32))
    part, sent = blocks_of(rows, step, start)
    part_ref[...] = part
    mate_ref[...] = sent[:shared]
    far_ref[...] = sent[shared:]


def keep(at, x, x_ref, high_ref, low_ref):
    x_ref[at, :] = x
    high_ref[at, :], low_ref[at, :] = halves(x)


def precondition_first(near_ref, r_ref, w_ref, rt_ref, m_ref, s_ref,
                       out_ref, mate_ref, far_ref, part_ref, total_ref, x_ref, high_ref, low_ref):
    total = summed(near_ref)
    total_ref[...] = total
    amounts = stacked(total)

    def step(at, i, carry):
        keep(at, w_ref[at, :] * (r_ref[at, :] - fast(rt_ref[at, :], amounts)), x_ref, high_ref, low_ref)
        return carry

    blocks_of(r_ref.shape[0], step, 0)
    multiply(m_ref, s_ref, x_ref, high_ref, low_ref, out_ref, mate_ref, far_ref, part_ref)


def direct_first(near_ref, v_ref, rt_ref, m_ref, s_ref,
                 out_ref, mate_ref, far_ref, part_ref, total_ref, x_ref, high_ref, low_ref):
    total = summed(near_ref)
    total_ref[...] = total
    amounts = stacked(total)

    def step(at, i, carry):
        keep(at, v_ref[at, :] - fast(rt_ref[at, :], amounts), x_ref, high_ref, low_ref)
        return carry

    blocks_of(v_ref.shape[0], step, 0)
    multiply(m_ref, s_ref, x_ref, high_ref, low_ref, out_ref, mate_ref, far_ref, part_ref)


def precondition_next(modes, near_ref, before_ref, norm_ref, r_ref, image_ref, w_ref, rt_ref, m_ref, s_ref,
                      out_ref, mate_ref, far_ref, part_ref, size_ref, r_out_ref, step_ref, x_ref, high_ref, low_ref):
    total = summed(near_ref)
    length = norm_ref[modes:modes + 1, :] / total[modes:modes + 1]
    step_ref[...] = length
    amounts = stacked(before_ref[...] - length * total)

    def step(at, i, size):
        residual = r_ref[at, :] - length * image_ref[at, :]
        r_out_ref[at, :] = residual
        weighted = w_ref[at, :] * residual
        keep(at, w_ref[at, :] * (residual - fast(rt_ref[at, :], amounts)), x_ref, high_ref, low_ref)
        return size + jnp.sum(weighted * residual, axis=0, keepdims=True)

    size_ref[...] = blocks_of(r_ref.shape[0], step, jnp.zeros((1, r_ref.shape[1]), F32))
    multiply(m_ref, s_ref, x_ref, high_ref, low_ref, out_ref, mate_ref, far_ref, part_ref)


def direct_next(modes, near_ref, norm_ref, v_ref, d_ref, rt_ref, m_ref, s_ref,
                out_ref, mate_ref, far_ref, part_ref, total_ref, x_ref, high_ref, low_ref):
    total = summed(near_ref)
    total_ref[...] = total
    ratio = total[modes:modes + 1] / norm_ref[modes:modes + 1, :]
    amounts = stacked(total)

    def step(at, i, carry):
        update = v_ref[at, :] - fast(rt_ref[at, :], amounts)
        keep(at, update + ratio * d_ref[at, :], x_ref, high_ref, low_ref)
        return carry

    blocks_of(v_ref.shape[0], step, 0)
    multiply(m_ref, s_ref, x_ref, high_ref, low_ref, out_ref, mate_ref, far_ref, part_ref)


def received(mate_ref, far_ref):
    return halves(jnp.concatenate([mate_ref[...], far_ref[...]], axis=0))


def pack_out(modes, pack_ref, sums, low_sums, first, second):
    part = sums[:TILE] + sums[TILE:] + low_sums[:TILE]
    row = lax.broadcasted_iota(jnp.int32, part.shape, 0)
    part = jnp.where(row == modes, first, jnp.where(row == modes + 1, second, part))
    for member in range(pack_ref.shape[0]):
        pack_ref[member] = part


def gather_modes(rigid_ref, value, i, sums, low_sums):
    zh, zl = halves(value)
    rigid = rigid_ref[i]
    return sums + fast(rigid, zh), low_sums + fast(rigid, zl)


def paired(value):
    high, low = halves(value)
    return jnp.concatenate([high.astype(F32), low.astype(F32)], axis=0).astype(BF16)


def folded(pair):
    return pair[:TILE] + pair[TILE:]


def prepare_body(modes, group, gap_ref, coarse_ref, rigid_ref, s_ref, mate_ref, far_ref, wide_ref):
    shared = s_ref.shape[1] // 2
    cases = gap_ref.shape[1]

    def step(at, i, sent):
        high, rest = halves(gap_ref[at, :])
        pick = s_ref[i]
        low = rest.astype(F32)
        tail = (gap_ref[at, :] - high.astype(F32) - low).astype(BF16)
        return sent + (fast(pick, high) + fast(pick, rest) + fast(pick, tail))

    sent = blocks_of(gap_ref.shape[0], step, jnp.zeros((2 * shared, cases), F32))
    mate_ref[:shared, :] = sent[:shared]
    far_ref[:shared, :] = sent[shared:]

    narrow, wide = 4 * group * modes, 4 * group * TILE
    column = lax.broadcasted_iota(jnp.int32, (narrow, wide), 1)
    source = (column // TILE) * modes + column % TILE
    source = jnp.where(column % TILE < modes, source, -1)
    widen = jnp.where(lax.broadcasted_iota(jnp.int32, (narrow, wide), 0) == source, 1.0, 0.0).astype(BF16)
    for part in range(coarse_ref.shape[1] // narrow):
        spread = folded(fast(paired(coarse_ref[:, part * narrow:(part + 1) * narrow]), widen))
        for piece in range(wide // cases):
            top = shared + TILE * (part * (wide // cases) + piece)
            value = spread[:, piece * cases:(piece + 1) * cases]
            mate_ref[top:top + TILE, :] = value
            far_ref[top:top + TILE, :] = value

    picked = jnp.zeros((2 * TILE, 2 * shared), F32)
    for i in range(s_ref.shape[0]):
        rigid = paired(rigid_ref[:, i * ROWS:(i + 1) * ROWS])
        wide_ref[i] = rigid
        picked = picked + lax.dot_general(
            rigid, s_ref[i], (((1,), (1,)), ((), ())), preferred_element_type=F32
        )
    picked = folded(picked)
    spare = jnp.zeros((TILE, cases - shared), F32)
    last = mate_ref.shape[0] - TILE
    mate_ref[last:, :] = jnp.concatenate([picked[:, :shared], spare], axis=1)
    far_ref[last:, :] = jnp.concatenate([picked[:, shared:], spare], axis=1)


def tile_body(modes, shared, own_ref, mate_ref, far_ref, out_ref):
    wide = out_ref.shape[2]
    row = lax.broadcasted_iota(jnp.int32, (TILE, wide), 0)
    column = lax.broadcasted_iota(jnp.int32, (TILE, wide), 1)
    ones = jnp.where((row >= modes) & (column % TILE == row), 1.0, 0.0)
    per_row = own_ref.shape[1] // wide
    for member in range(out_ref.shape[0]):
        top = shared + TILE * (member // per_row)
        left = wide * (member % per_row)
        at = (slice(top, top + TILE), slice(left, left + wide))
        out_ref[member, :TILE, :] = own_ref[at] + ones
        out_ref[member, TILE:2 * TILE, :] = mate_ref[at]
        out_ref[member, 2 * TILE:, :] = far_ref[at]


def start_body(modes, y_ref, mate_ref, far_ref, st_ref, w_ref, wide_ref, out_ref, pack_ref, tall_ref):
    shared = st_ref.shape[1] // 2
    cases = y_ref.shape[1]
    rows = jnp.concatenate([mate_ref[:shared, :], far_ref[:shared, :]], axis=0)
    rh, rest = halves(rows)
    rt = (rows - rh.astype(F32) - rest.astype(F32)).astype(BF16)
    last = mate_ref.shape[0] - TILE
    near_mate = paired(mate_ref[last:, :shared])
    near_far = paired(far_ref[last:, :shared])
    spare = jnp.zeros((TILE, ROWS), F32)

    def step(at, i, carry):
        size, sums, low_sums = carry
        place = st_ref[at, :]
        value = y_ref[at, :] + (fast(place, rh) + fast(place, rest) + fast(place, rt))
        out_ref[at, :] = value
        size = size + jnp.sum(w_ref[at, :] * value * value, axis=0, keepdims=True)

        def across(near, hot):
            return folded(lax.dot_general(near, hot, (((1,), (1,)), ((), ())), preferred_element_type=F32))

        own = folded(wide_ref[i].astype(F32))
        stack = jnp.concatenate(
            [own, across(near_mate, place[:, :shared]), across(near_far, place[:, shared:]), spare], axis=0
        )
        high, low = halves(stack)
        high, low = high.astype(F32), low.astype(F32)
        stack = jnp.concatenate([high, high, low, jnp.zeros_like(low)], axis=0)
        tall_ref[at, :] = stack.T.astype(BF16)
        return (size, *gather_modes(wide_ref, value, i, sums, low_sums))

    zeros = jnp.zeros((2 * TILE, cases), F32)
    size, sums, low_sums = blocks_of(y_ref.shape[0], step, (jnp.zeros((1, cases), F32), zeros, zeros))
    pack_out(modes, pack_ref, sums, low_sums, size, jnp.zeros_like(size))


def assemble_body(modes, weighted, sized, *refs):
    y_ref, mate_ref, far_ref, st_ref, rigid_ref, part_ref = refs[:6]
    w_ref = refs[6] if weighted else None
    size_ref = refs[6 + weighted] if sized else None
    out_ref, pack_ref = refs[6 + weighted + sized:]
    rh, rl = received(mate_ref, far_ref)

    def step(at, i, carry):
        place = st_ref[at, :]
        value = y_ref[at, :] + (fast(place, rh) + fast(place, rl))
        if weighted:
            value = w_ref[at, :] * value
        out_ref[at, :] = value
        return gather_modes(rigid_ref, value, i, *carry)

    zeros = jnp.zeros((2 * TILE, y_ref.shape[1]), F32)
    sums, low_sums = blocks_of(y_ref.shape[0], step, (zeros, zeros))
    part = part_ref[...]
    pack_out(modes, pack_ref, sums, low_sums, part, size_ref[...] if sized else jnp.zeros_like(part))


def block_body(block_ref, near_ref, out_ref):
    members, tile, cases = near_ref.shape
    high, low = halves(near_ref[...].reshape(members * tile, cases))
    outer, tall, wide = block_ref.shape
    block_high, block_low = halves(block_ref[...].reshape(outer * tall, wide))
    block = jnp.concatenate([block_high, block_high, block_low], axis=1)
    out = fast(block, jnp.concatenate([high, low, high], axis=0))
    out_ref[...] = out.reshape(out_ref.shape)


def finish_body(q_ref, mate_ref, far_ref, st_ref, r_ref, first_ref, second_ref, step_first_ref, step_ref,
                multipliers_ref, residual_ref):
    rh, rl = received(mate_ref, far_ref)
    first, second = step_first_ref[...], step_ref[...]

    def step(at, i, carry):
        place = st_ref[at, :]
        image = q_ref[at, :] + (fast(place, rh) + fast(place, rl))
        multipliers_ref[at, :] = first * first_ref[at, :] + second * second_ref[at, :]
        residual_ref[at, :] = r_ref[at, :] - second * image
        return carry

    blocks_of(q_ref.shape[0], step, 0)


def shards(dual_ops, boundary_solve_blocks, rigid_images, coarse_rows, gap_raw, row_maps):
    modes, local_rows = rigid_images.shape
    cases = gap_raw.shape[1]
    count = lax.axis_size(CLUSTER_SUB)
    outer, inner = lax.axis_size(OUTER), lax.axis_size(INNER)
    place = lax.axis_index(CLUSTER_SUB)
    even = place % 2 == 0
    inside = jnp.where((place > 0) & (place < count - 1), 1.0, 0.0).astype(F32)
    mate = jnp.where(even, row_maps[0, 1], row_maps[0, 0])
    far = jnp.where(even, row_maps[0, 0], row_maps[0, 1])
    shared = mate.shape[0]
    mate_pairs, far_pairs = matchings(count)

    def exchanged(to_mate, to_far):
        from_far = matched(to_far, far_pairs)
        from_mate = matched(to_mate, mate_pairs)
        return from_mate, from_far

    picks = jnp.concatenate([mate, far])
    live = jnp.concatenate([jnp.ones((shared,), F32), jnp.full((shared,), inside)])
    blocks = (local_rows // ROWS, 2 * shared, ROWS)
    numbers = lax.broadcasted_iota(jnp.int32, blocks, 0) * ROWS + lax.broadcasted_iota(jnp.int32, blocks, 2)
    selector = jnp.where(picks[None, :, None] == numbers, live[None, :, None], 0.0).astype(BF16)
    placer = jnp.where(
        picks[None, :] == lax.broadcasted_iota(jnp.int32, (local_rows, 2 * shared), 0), live[None, :], 0.0
    )
    weights = jnp.broadcast_to(1.0 - 0.5 * jnp.sum(placer, axis=1, keepdims=True), (local_rows, cases))
    placer = placer.astype(BF16)

    field = (local_rows, cases)
    edge = (shared, cases)
    row = (1, cases)
    rows_out = (3 * TILE, cases)
    pack_shape = (inner, TILE, cases)
    scratch = [pltpu.VMEM(field, F32), pltpu.VMEM(field, BF16), pltpu.VMEM(field, BF16)]
    own = scratch[1:]
    big = 6 * local_rows * local_rows * cases
    light = 4 * local_rows * cases * 2 * shared
    moved = 4 * local_rows * (local_rows + 3 * cases)

    def shaped(shape, dtype):
        return jax.ShapeDtypeStruct(shape, dtype)

    pad = ((0, TILE - modes), (0, 0))
    payload = (shared + TILE * (outer * inner * TILE // cases) + TILE, cases)
    to_mate, to_far, rigid_wide = call(
        functools.partial(prepare_body, modes, inner),
        [payload, payload, shaped((local_rows // ROWS, 2 * TILE, ROWS), BF16)], [], light, 8 * local_rows * cases,
    )(gap_raw, jnp.pad(coarse_rows, pad), jnp.pad(rigid_images, pad), selector)
    from_mate, from_far = exchanged(to_mate, to_far)
    from_mate, from_far, placer, weights = lax.optimization_barrier((from_mate, from_far, placer, weights))
    [block] = call(
        functools.partial(tile_body, modes, shared), [(outer, 3 * TILE, inner * TILE)], [], 1, 8 * local_rows
    )(to_mate, from_mate, from_far)
    block = swap(block, OUTER)
    block, from_mate, from_far, placer, weights = lax.optimization_barrier(
        (block, from_mate, from_far, placer, weights)
    )

    def coarse(pack):
        near = swap(pack, INNER)
        [rows] = call(block_body, [(outer, 3 * TILE, cases)], [], 6 * outer * 3 * TILE * inner * TILE * cases,
                      4 * outer * 4 * TILE * cases)(block, near)
        return swap(rows, OUTER)

    def assemble(weighted, sized, *operands):
        body = functools.partial(assemble_body, modes, weighted, sized)
        return call(body, [field, pack_shape], [], light, 12 * local_rows * cases)(*operands)

    residual, pack, rigid_tall = call(
        functools.partial(start_body, modes), [field, pack_shape, shaped((local_rows, 128), BF16)], [], light,
        12 * local_rows * cases,
    )(gap_raw, from_mate, from_far, placer, weights, rigid_wide)
    near = coarse(pack)
    out, to_mate, to_far, part, amounts = call(
        precondition_first, [field, edge, edge, row, rows_out], scratch, big, moved
    )(near, residual, weights, rigid_tall, boundary_solve_blocks, selector)
    norm_first = amounts[modes]
    smoothed, pack = assemble(True, False, out, *exchanged(to_mate, to_far), placer, rigid_wide, part, weights)
    near = coarse(pack)
    out, to_mate, to_far, part, total, direction_first = call(
        direct_first, [field, edge, edge, row, rows_out, field], own, big, moved
    )(near, smoothed, rigid_tall, dual_ops, selector)
    image, pack = assemble(False, False, out, *exchanged(to_mate, to_far), placer, rigid_wide, part)
    near = coarse(pack)
    out, to_mate, to_far, part, size, residual, step_first = call(
        functools.partial(precondition_next, modes), [field, edge, edge, row, row, field, row], scratch, big, moved
    )(near, amounts, total, residual, image, weights, rigid_tall, boundary_solve_blocks, selector)
    smoothed, pack = assemble(True, True, out, *exchanged(to_mate, to_far), placer, rigid_wide, part, weights, size)
    near = coarse(pack)
    out, to_mate, to_far, part, last, direction = call(
        functools.partial(direct_next, modes), [field, edge, edge, row, rows_out, field], own, big, moved
    )(near, total, smoothed, direction_first, rigid_tall, dual_ops, selector)
    norms = jnp.stack([norm_first, last[modes + 1]])
    from_mate, from_far = exchanged(to_mate, to_far)
    part, from_mate, from_far, norms = lax.optimization_barrier((part, from_mate, from_far, norms))
    bending = jnp.sum(swap(jnp.broadcast_to(part, (count, 1, cases)), CLUSTER_SUB), axis=0)
    step = last[modes:modes + 1] / bending
    multipliers, residual = call(finish_body, [field, field], [], light, 24 * local_rows * cases)(
        out, from_mate, from_far, placer, residual, direction_first, direction, step_first, step
    )
    return (multipliers, residual, norms)


def solution(mesh):
    devices = mesh.devices
    x, sub = devices.shape
    split = Mesh(devices.reshape(x, 4, sub // 8, 2), CLUSTER_SUB)
    in_specs = (P(CLUSTER_SUB, None),) * 5 + (P(CLUSTER_SUB, None, None),)
    out_specs = (P(CLUSTER_SUB, None), P(CLUSTER_SUB, None), P())
    return jax.shard_map(
        shards, mesh=split, in_specs=in_specs, out_specs=out_specs, check_vma=False
    )
```

```python
import functools

import jax
import jax.numpy as jnp
from jax import lax
from jax.experimental import pallas as pl
from jax.experimental.pallas import tpu as pltpu
from jax.sharding import Mesh
from jax.sharding import PartitionSpec as P

CLUSTER_SUB = ("cluster", "sub_0", "sub_1", "sub_2")
OUTER = ("cluster", "sub_0")
INNER = ("sub_1", "sub_2")
TILE = 8
ROWS = 256
VMEM_LIMIT = 24 * 1024 * 1024

F32 = jnp.float32
BF16 = jnp.bfloat16


def fast(a, b):
    return jnp.dot(a, b, preferred_element_type=F32)


def halves(value):
    high = value.astype(BF16)
    return high, (value - high.astype(F32)).astype(BF16)


def swap(blocks, axis):
    return lax.all_to_all(blocks, axis, split_axis=0, concat_axis=0, tiled=True)


def matched(value, pairs):
    return lax.ppermute(value, CLUSTER_SUB, pairs)


def matchings(count):
    near = [(i, i ^ 1) for i in range(count)]
    far = [(i, (((i + 1) ^ 1) - 1) % count) for i in range(count)]
    return near, far


def call(body, out_shapes, scratch, flops, moved):
    def run(*operands):
        return pl.pallas_call(
            body,
            out_shape=[s if hasattr(s, "dtype") else jax.ShapeDtypeStruct(s, F32) for s in out_shapes],
            in_specs=[pl.BlockSpec(memory_space=pltpu.VMEM)] * len(operands),
            out_specs=[pl.BlockSpec(memory_space=pltpu.VMEM)] * len(out_shapes),
            scratch_shapes=scratch,
            compiler_params=pltpu.CompilerParams(vmem_limit_bytes=VMEM_LIMIT),
            cost_estimate=pl.CostEstimate(flops=flops, bytes_accessed=moved, transcendentals=0),
        )(*operands)

    return run


def summed(near_ref):
    total = near_ref[0]
    for member in range(1, near_ref.shape[0]):
        total = total + near_ref[member]
    return total


def stacked(amounts):
    spare = jnp.zeros((TILE, amounts.shape[1]), F32)
    high, low = halves(jnp.concatenate([amounts, spare], axis=0))
    return jnp.concatenate([high, low, high, jnp.zeros_like(high)], axis=0)


def blocks_of(rows, body, start):
    return lax.fori_loop(0, rows // ROWS, lambda i, c: body(pl.ds(pl.multiple_of(i * ROWS, ROWS), ROWS), i, c), start)


def pick_body(m_ref, s_ref, high_ref, low_ref):
    def step(j, carry):
        at = pl.ds(pl.multiple_of(j * ROWS, ROWS), ROWS)
        rows = jnp.zeros((s_ref.shape[1], ROWS), F32)
        for i in range(s_ref.shape[0]):
            part = m_ref[i * ROWS:(i + 1) * ROWS, at]
            high, low = halves(part)
            tail = (part - high.astype(F32) - low.astype(F32)).astype(BF16)
            pick = s_ref[i]
            rows = rows + (fast(pick, high) + fast(pick, low) + fast(pick, tail))
        high_ref[:, at], low_ref[:, at] = halves(rows)
        return carry

    lax.fori_loop(0, m_ref.shape[1] // ROWS, step, 0)


def multiply_body(m_ref, x_ref, high_ref, low_ref, out_ref, part_ref):
    xh, xl = high_ref[...], low_ref[...]

    def step(at, i, part):
        mh, ml = halves(m_ref[at, :])
        out = fast(mh, xh) + fast(mh, xl) + fast(ml, xh)
        out_ref[at, :] = out
        return part + jnp.sum(x_ref[at, :] * out, axis=0, keepdims=True)

    part = blocks_of(out_ref.shape[0], step, jnp.zeros((1, out_ref.shape[1]), F32))
    copied(part_ref, part)


def copied(ref, row):
    if len(ref.shape) == 2:
        ref[...] = row
        return
    for member in range(ref.shape[0]):
        ref[member] = row


def relay_body(near_ref, out_ref):
    copied(out_ref, summed(near_ref))


def keep(at, x, outs):
    x_ref, high_ref, low_ref = outs[2:5]
    x_ref[at, :] = x
    high_ref[at, :], low_ref[at, :] = halves(x)


def send(edge_high_ref, edge_low_ref, outs):
    mate_ref, far_ref, _, high_ref, low_ref = outs[:5]
    xh, xl, mh = high_ref[...], low_ref[...], edge_high_ref[...]
    sent = fast(mh, xh) + fast(mh, xl) + fast(edge_low_ref[...], xh)
    shared = mate_ref.shape[0]
    mate_ref[...] = sent[:shared]
    far_ref[...] = sent[shared:]


def precondition_first(near_ref, edge_high_ref, edge_low_ref, rt_ref, r_ref, w_ref, *outs):
    total = summed(near_ref)
    outs[5][...] = total
    amounts = stacked(total)

    def step(at, i, carry):
        keep(at, w_ref[at, :] * (r_ref[at, :] - fast(rt_ref[at, :], amounts)), outs)
        return carry

    blocks_of(r_ref.shape[0], step, 0)
    send(edge_high_ref, edge_low_ref, outs)


def direct_first(near_ref, edge_high_ref, edge_low_ref, rt_ref, v_ref, *outs):
    total = summed(near_ref)
    outs[5][...] = total
    amounts = stacked(total)

    def step(at, i, carry):
        keep(at, v_ref[at, :] - fast(rt_ref[at, :], amounts), outs)
        return carry

    blocks_of(v_ref.shape[0], step, 0)
    send(edge_high_ref, edge_low_ref, outs)


def precondition_next(modes, near_ref, edge_high_ref, edge_low_ref, rt_ref, before_ref, norm_ref, r_ref, image_ref,
                      w_ref, *outs):
    size_ref, r_out_ref, step_ref = outs[5:]
    total = summed(near_ref)
    length = norm_ref[modes:modes + 1, :] / total[modes:modes + 1]
    step_ref[...] = length
    amounts = stacked(before_ref[...] - length * total)

    def step(at, i, size):
        residual = r_ref[at, :] - length * image_ref[at, :]
        r_out_ref[at, :] = residual
        weighted = w_ref[at, :] * residual
        keep(at, w_ref[at, :] * (residual - fast(rt_ref[at, :], amounts)), outs)
        return size + jnp.sum(weighted * residual, axis=0, keepdims=True)

    size_ref[...] = blocks_of(r_ref.shape[0], step, jnp.zeros((1, r_ref.shape[1]), F32))
    send(edge_high_ref, edge_low_ref, outs)


def direct_next(modes, near_ref, edge_high_ref, edge_low_ref, rt_ref, norm_ref, first_ref, v_ref, d_ref, *outs):
    total = summed(near_ref)
    outs[5][...] = total
    outs[6][0:1, :] = first_ref[modes:modes + 1, :]
    outs[6][1:2, :] = total[modes + 1:modes + 2]
    ratio = total[modes:modes + 1] / norm_ref[modes:modes + 1, :]
    amounts = stacked(total)

    def step(at, i, carry):
        update = v_ref[at, :] - fast(rt_ref[at, :], amounts)
        keep(at, update + ratio * d_ref[at, :], outs)
        return carry

    blocks_of(v_ref.shape[0], step, 0)
    send(edge_high_ref, edge_low_ref, outs)


def received(mate_ref, far_ref):
    return halves(jnp.concatenate([mate_ref[...], far_ref[...]], axis=0))


def pack_out(modes, pack_ref, sums, low_sums, first, second):
    part = sums[:TILE] + sums[TILE:] + low_sums[:TILE]
    row = lax.broadcasted_iota(jnp.int32, part.shape, 0)
    part = jnp.where(row == modes, first, jnp.where(row == modes + 1, second, part))
    for member in range(pack_ref.shape[0]):
        pack_ref[member] = part


def gather_modes(rigid_ref, value, i, sums, low_sums):
    zh, zl = halves(value)
    rigid = rigid_ref[i]
    return sums + fast(rigid, zh), low_sums + fast(rigid, zl)


def paired(value):
    high, low = halves(value)
    return jnp.concatenate([high.astype(F32), low.astype(F32)], axis=0).astype(BF16)


def folded(pair):
    return pair[:TILE] + pair[TILE:]


def prepare_body(modes, group, gap_ref, coarse_ref, rigid_ref, s_ref, mate_ref, far_ref, wide_ref):
    shared = s_ref.shape[1] // 2
    cases = gap_ref.shape[1]

    def step(at, i, sent):
        high, rest = halves(gap_ref[at, :])
        pick = s_ref[i]
        low = rest.astype(F32)
        tail = (gap_ref[at, :] - high.astype(F32) - low).astype(BF16)
        return sent + (fast(pick, high) + fast(pick, rest) + fast(pick, tail))

    sent = blocks_of(gap_ref.shape[0], step, jnp.zeros((2 * shared, cases), F32))
    mate_ref[:shared, :] = sent[:shared]
    far_ref[:shared, :] = sent[shared:]

    narrow, wide = 4 * group * modes, 4 * group * TILE
    column = lax.broadcasted_iota(jnp.int32, (narrow, wide), 1)
    source = (column // TILE) * modes + column % TILE
    source = jnp.where(column % TILE < modes, source, -1)
    widen = jnp.where(lax.broadcasted_iota(jnp.int32, (narrow, wide), 0) == source, 1.0, 0.0).astype(BF16)
    for part in range(coarse_ref.shape[1] // narrow):
        spread = folded(fast(paired(coarse_ref[:, part * narrow:(part + 1) * narrow]), widen))
        for piece in range(wide // cases):
            top = shared + TILE * (part * (wide // cases) + piece)
            value = spread[:, piece * cases:(piece + 1) * cases]
            mate_ref[top:top + TILE, :] = value
            far_ref[top:top + TILE, :] = value

    picked = jnp.zeros((2 * TILE, 2 * shared), F32)
    for i in range(s_ref.shape[0]):
        rigid = paired(rigid_ref[:, i * ROWS:(i + 1) * ROWS])
        wide_ref[i] = rigid
        picked = picked + lax.dot_general(
            rigid, s_ref[i], (((1,), (1,)), ((), ())), preferred_element_type=F32
        )
    picked = folded(picked)
    spare = jnp.zeros((TILE, cases - shared), F32)
    last = mate_ref.shape[0] - TILE
    mate_ref[last:, :] = jnp.concatenate([picked[:, :shared], spare], axis=1)
    far_ref[last:, :] = jnp.concatenate([picked[:, shared:], spare], axis=1)


def tile_body(modes, shared, own_ref, mate_ref, far_ref, out_ref):
    wide = out_ref.shape[2]
    row = lax.broadcasted_iota(jnp.int32, (TILE, wide), 0)
    column = lax.broadcasted_iota(jnp.int32, (TILE, wide), 1)
    ones = jnp.where((row >= modes) & (column % TILE == row), 1.0, 0.0)
    per_row = own_ref.shape[1] // wide
    for member in range(out_ref.shape[0]):
        top = shared + TILE * (member // per_row)
        left = wide * (member % per_row)
        at = (slice(top, top + TILE), slice(left, left + wide))
        out_ref[member, :TILE, :] = own_ref[at] + ones
        out_ref[member, TILE:2 * TILE, :] = mate_ref[at]
        out_ref[member, 2 * TILE:, :] = far_ref[at]


def start_body(modes, y_ref, mate_ref, far_ref, st_ref, w_ref, wide_ref, out_ref, pack_ref, tall_ref):
    shared = st_ref.shape[1] // 2
    cases = y_ref.shape[1]
    rows = jnp.concatenate([mate_ref[:shared, :], far_ref[:shared, :]], axis=0)
    rh, rest = halves(rows)
    rt = (rows - rh.astype(F32) - rest.astype(F32)).astype(BF16)
    last = mate_ref.shape[0] - TILE
    near_mate = paired(mate_ref[last:, :shared])
    near_far = paired(far_ref[last:, :shared])
    spare = jnp.zeros((TILE, ROWS), F32)

    def step(at, i, carry):
        size, sums, low_sums = carry
        place = st_ref[at, :]
        value = y_ref[at, :] + (fast(place, rh) + fast(place, rest) + fast(place, rt))
        out_ref[at, :] = value
        size = size + jnp.sum(w_ref[at, :] * value * value, axis=0, keepdims=True)

        def across(near, hot):
            return folded(lax.dot_general(near, hot, (((1,), (1,)), ((), ())), preferred_element_type=F32))

        own = folded(wide_ref[i].astype(F32))
        stack = jnp.concatenate(
            [own, across(near_mate, place[:, :shared]), across(near_far, place[:, shared:]), spare], axis=0
        )
        high, low = halves(stack)
        high, low = high.astype(F32), low.astype(F32)
        stack = jnp.concatenate([high, high, low, jnp.zeros_like(low)], axis=0)
        tall_ref[at, :] = stack.T.astype(BF16)
        return (size, *gather_modes(wide_ref, value, i, sums, low_sums))

    zeros = jnp.zeros((2 * TILE, cases), F32)
    size, sums, low_sums = blocks_of(y_ref.shape[0], step, (jnp.zeros((1, cases), F32), zeros, zeros))
    pack_out(modes, pack_ref, sums, low_sums, size, jnp.zeros_like(size))


def assemble_body(modes, weighted, sized, *refs):
    y_ref, mate_ref, far_ref, st_ref, rigid_ref, part_ref = refs[:6]
    w_ref = refs[6] if weighted else None
    size_ref = refs[6 + weighted] if sized else None
    out_ref, pack_ref = refs[6 + weighted + sized:]
    rh, rl = received(mate_ref, far_ref)

    def step(at, i, carry):
        place = st_ref[at, :]
        value = y_ref[at, :] + (fast(place, rh) + fast(place, rl))
        if weighted:
            value = w_ref[at, :] * value
        out_ref[at, :] = value
        return gather_modes(rigid_ref, value, i, *carry)

    zeros = jnp.zeros((2 * TILE, y_ref.shape[1]), F32)
    sums, low_sums = blocks_of(y_ref.shape[0], step, (zeros, zeros))
    part = part_ref[...]
    pack_out(modes, pack_ref, sums, low_sums, part, size_ref[...] if sized else jnp.zeros_like(part))


def block_body(block_ref, near_ref, out_ref):
    members, tile, cases = near_ref.shape
    high, low = halves(near_ref[...].reshape(members * tile, cases))
    outer, tall, wide = block_ref.shape
    block_high, block_low = halves(block_ref[...].reshape(outer * tall, wide))
    block = jnp.concatenate([block_high, block_high, block_low], axis=1)
    out = fast(block, jnp.concatenate([high, low, high], axis=0))
    out_ref[...] = out.reshape(out_ref.shape)


def finish_body(modes, q_ref, mate_ref, far_ref, st_ref, r_ref, first_ref, second_ref, step_first_ref, last_ref,
                bending_ref, multipliers_ref, residual_ref):
    rh, rl = received(mate_ref, far_ref)
    first = step_first_ref[...]
    second = last_ref[modes:modes + 1, :] / summed(bending_ref)

    def step(at, i, carry):
        place = st_ref[at, :]
        image = q_ref[at, :] + (fast(place, rh) + fast(place, rl))
        multipliers_ref[at, :] = first * first_ref[at, :] + second * second_ref[at, :]
        residual_ref[at, :] = r_ref[at, :] - second * image
        return carry

    blocks_of(q_ref.shape[0], step, 0)


def shards(dual_ops, boundary_solve_blocks, rigid_images, coarse_rows, gap_raw, row_maps):
    modes, local_rows = rigid_images.shape
    cases = gap_raw.shape[1]
    count = lax.axis_size(CLUSTER_SUB)
    outer, inner = lax.axis_size(OUTER), lax.axis_size(INNER)
    place = lax.axis_index(CLUSTER_SUB)
    even = place % 2 == 0
    inside = jnp.where((place > 0) & (place < count - 1), 1.0, 0.0).astype(F32)
    mate = jnp.where(even, row_maps[0, 1], row_maps[0, 0])
    far = jnp.where(even, row_maps[0, 0], row_maps[0, 1])
    shared = mate.shape[0]
    mate_pairs, far_pairs = matchings(count)

    def exchanged(to_mate, to_far):
        from_far = matched(to_far, far_pairs)
        from_mate = matched(to_mate, mate_pairs)
        return from_mate, from_far

    picks = jnp.concatenate([mate, far])
    live = jnp.concatenate([jnp.ones((shared,), F32), jnp.full((shared,), inside)])
    blocks = (local_rows // ROWS, 2 * shared, ROWS)
    numbers = lax.broadcasted_iota(jnp.int32, blocks, 0) * ROWS + lax.broadcasted_iota(jnp.int32, blocks, 2)
    selector = jnp.where(picks[None, :, None] == numbers, live[None, :, None], 0.0).astype(BF16)
    placer = jnp.where(
        picks[None, :] == lax.broadcasted_iota(jnp.int32, (local_rows, 2 * shared), 0), live[None, :], 0.0
    )
    weights = jnp.broadcast_to(1.0 - 0.5 * jnp.sum(placer, axis=1, keepdims=True), (local_rows, cases))
    placer = placer.astype(BF16)

    field = (local_rows, cases)
    edge = (shared, cases)
    row = (1, cases)
    rows_out = (3 * TILE, cases)
    pack_shape = (inner, TILE, cases)
    big = 6 * local_rows * local_rows * cases
    light = 4 * local_rows * cases * 2 * shared
    moved = 4 * local_rows * (local_rows + 3 * cases)

    def shaped(shape, dtype):
        return jax.ShapeDtypeStruct(shape, dtype)

    pad = ((0, TILE - modes), (0, 0))
    payload = (shared + TILE * (outer * inner * TILE // cases) + TILE, cases)
    to_mate, to_far, rigid_wide = call(
        functools.partial(prepare_body, modes, inner),
        [payload, payload, shaped((local_rows // ROWS, 2 * TILE, ROWS), BF16)], [], light, 8 * local_rows * cases,
    )(gap_raw, jnp.pad(coarse_rows, pad), jnp.pad(rigid_images, pad), selector)
    from_mate, from_far = exchanged(to_mate, to_far)
    edges = [
        call(pick_body, [shaped((2 * shared, local_rows), BF16)] * 2, [], light, 4 * local_rows * local_rows)(m, selector)
        for m in (boundary_solve_blocks, dual_ops)
    ]
    from_mate, from_far, placer, weights, edges = lax.optimization_barrier(
        (from_mate, from_far, placer, weights, edges)
    )
    [block] = call(
        functools.partial(tile_body, modes, shared), [(outer, 3 * TILE, inner * TILE)], [], 1, 8 * local_rows
    )(to_mate, from_mate, from_far)
    block = swap(block, OUTER)
    block, from_mate, from_far, placer, weights, edges = lax.optimization_barrier(
        (block, from_mate, from_far, placer, weights, edges)
    )

    def coarse(pack):
        near = swap(pack, INNER)
        [rows] = call(block_body, [(outer, 3 * TILE, cases)], [], 6 * outer * 3 * TILE * inner * TILE * cases,
                      4 * outer * 4 * TILE * cases)(block, near)
        return swap(rows, OUTER)

    def assemble(weighted, sized, *operands):
        body = functools.partial(assemble_body, modes, weighted, sized)
        return call(body, [field, pack_shape], [], light, 12 * local_rows * cases)(*operands)

    residual, pack, rigid_tall = call(
        functools.partial(start_body, modes), [field, pack_shape, shaped((local_rows, 128), BF16)], [], light,
        12 * local_rows * cases,
    )(gap_raw, from_mate, from_far, placer, weights, rigid_wide)
    sent = [edge, edge, field, shaped(field, BF16), shaped(field, BF16)]

    def advance(body, extra, near, which, *operands, parts=row):
        to_mate, to_far, x, high, low, *rest = call(
            body, sent + extra, [], light, 12 * local_rows * cases
        )(near, *edges[which], rigid_tall, *operands)
        out, part = call(multiply_body, [field, parts], [], big, moved)(
            (boundary_solve_blocks, dual_ops)[which], x, high, low
        )
        return out, exchanged(to_mate, to_far), part, x, *rest

    near = coarse(pack)
    out, received_rows, part, _, amounts = advance(precondition_first, [rows_out], near, 0, residual, weights)
    smoothed, pack = assemble(True, False, out, *received_rows, placer, rigid_wide, part, weights)
    near = coarse(pack)
    out, received_rows, part, direction_first, total = advance(direct_first, [rows_out], near, 1, smoothed)
    image, pack = assemble(False, False, out, *received_rows, placer, rigid_wide, part)
    near = coarse(pack)
    out, received_rows, part, _, size, residual, step_first = advance(
        functools.partial(precondition_next, modes), [row, field, row], near, 0, amounts, total, residual, image, weights
    )
    smoothed, pack = assemble(True, True, out, *received_rows, placer, rigid_wide, part, weights, size)
    near = coarse(pack)
    out, (from_mate, from_far), part, direction, last, norms = advance(
        functools.partial(direct_next, modes), [rows_out, (2, cases)], near, 1, total, amounts, smoothed, direction_first,
        parts=(inner, 1, cases),
    )
    part, norms, from_mate, from_far = lax.optimization_barrier((part, norms, from_mate, from_far))
    [part] = call(relay_body, [(outer, 1, cases)], [], 1, 4 * outer * cases)(swap(part, INNER))
    bending = swap(part, OUTER)
    multipliers, residual = call(functools.partial(finish_body, modes), [field, field], [], light, 24 * local_rows * cases)(
        out, from_mate, from_far, placer, residual, direction_first, direction, step_first, last, bending
    )
    return (multipliers, residual, norms)


def solution(mesh):
    devices = mesh.devices
    x, sub = devices.shape
    split = Mesh(devices.reshape(x, 4, sub // 8, 2), CLUSTER_SUB)
    in_specs = (P(CLUSTER_SUB, None),) * 5 + (P(CLUSTER_SUB, None, None),)
    out_specs = (P(CLUSTER_SUB, None), P(CLUSTER_SUB, None), P())
    return jax.shard_map(
        shards, mesh=split, in_specs=in_specs, out_specs=out_specs, check_vma=False
    )
```

```python
import functools

import jax
import jax.numpy as jnp
from jax import lax
from jax.experimental import pallas as pl
from jax.experimental.pallas import tpu as pltpu
from jax.sharding import Mesh
from jax.sharding import PartitionSpec as P

CLUSTER_SUB = ("cluster", "sub_0", "sub_1", "sub_2")
OUTER = ("cluster", "sub_0")
INNER = ("sub_1", "sub_2")
TILE = 8
ROWS = 256
VMEM_LIMIT = 24 * 1024 * 1024
LARGE_LIMIT = 66000000

F32 = jnp.float32
BF16 = jnp.bfloat16


def fast(a, b):
    return jnp.dot(a, b, preferred_element_type=F32)


def halves(value):
    high = value.astype(BF16)
    return high, (value - high.astype(F32)).astype(BF16)


def swap(blocks, axis):
    return lax.all_to_all(blocks, axis, split_axis=0, concat_axis=0, tiled=True)


def matched(value, pairs):
    return lax.ppermute(value, CLUSTER_SUB, pairs)


def matchings(count):
    near = [(i, i ^ 1) for i in range(count)]
    far = [(i, (((i + 1) ^ 1) - 1) % count) for i in range(count)]
    return near, far


def call(body, out_shapes, scratch, flops, moved, outside=0, limit=VMEM_LIMIT):
    def run(*operands):
        return pl.pallas_call(
            body,
            out_shape=[s if hasattr(s, "dtype") else jax.ShapeDtypeStruct(s, F32) for s in out_shapes],
            in_specs=[pl.BlockSpec(memory_space=pltpu.HBM)] * outside
            + [pl.BlockSpec(memory_space=pltpu.VMEM)] * (len(operands) - outside),
            out_specs=[pl.BlockSpec(memory_space=pltpu.VMEM)] * len(out_shapes),
            scratch_shapes=scratch,
            compiler_params=pltpu.CompilerParams(vmem_limit_bytes=limit),
            cost_estimate=pl.CostEstimate(flops=flops, bytes_accessed=moved, transcendentals=0),
        )(*operands)

    return run


def summed(near_ref):
    total = near_ref[0]
    for member in range(1, near_ref.shape[0]):
        total = total + near_ref[member]
    return total


def stacked(amounts):
    spare = jnp.zeros((TILE, amounts.shape[1]), F32)
    high, low = halves(jnp.concatenate([amounts, spare], axis=0))
    return jnp.concatenate([high, low, high, jnp.zeros_like(high)], axis=0)


def blocks_of(rows, body, start):
    return lax.fori_loop(0, rows // ROWS, lambda i, c: body(pl.ds(pl.multiple_of(i * ROWS, ROWS), ROWS), i, c), start)


def pick_body(m_ref, s_ref, high_ref, low_ref):
    def step(j, carry):
        at = pl.ds(pl.multiple_of(j * ROWS, ROWS), ROWS)
        rows = rest = jnp.zeros((s_ref.shape[1], ROWS), F32)
        for i in range(s_ref.shape[0]):
            high, low = halves(m_ref[i * ROWS:(i + 1) * ROWS, at])
            pick = s_ref[i]
            rows, rest = rows + fast(pick, high), rest + fast(pick, low)
        high_ref[:, at], low_ref[:, at] = rows.astype(BF16), rest.astype(BF16)
        return carry

    lax.fori_loop(0, m_ref.shape[1] // ROWS, step, 0)


def multiply_body(m_ref, x_ref, high_ref, low_ref, out_ref, part_ref):
    xh, xl = high_ref[...], low_ref[...]

    def step(at, i, part):
        mh, ml = halves(m_ref[at, :])
        out = fast(mh, xh) + fast(mh, xl) + fast(ml, xh)
        out_ref[at, :] = out
        return part + jnp.sum(x_ref[at, :] * out, axis=0, keepdims=True)

    part = blocks_of(out_ref.shape[0], step, jnp.zeros((1, out_ref.shape[1]), F32))
    copied(part_ref, part)


def copied(ref, row):
    if len(ref.shape) == 2:
        ref[...] = row
        return
    for member in range(ref.shape[0]):
        ref[member] = row


def relay_body(near_ref, out_ref):
    copied(out_ref, summed(near_ref))


def keep(at, x, outs):
    x_ref, high_ref, low_ref = outs[2:5]
    x_ref[at, :] = x
    high_ref[at, :], low_ref[at, :] = halves(x)


def send(edge_high_ref, edge_low_ref, outs):
    mate_ref, far_ref, _, high_ref, low_ref = outs[:5]
    xh, xl, mh = high_ref[...], low_ref[...], edge_high_ref[...]
    sent = fast(mh, xh) + fast(mh, xl) + fast(edge_low_ref[...], xh)
    shared = mate_ref.shape[0]
    mate_ref[...] = sent[:shared]
    far_ref[...] = sent[shared:]


def precondition_first(near_ref, edge_high_ref, edge_low_ref, rt_ref, r_ref, w_ref, *outs):
    total = summed(near_ref)
    outs[5][...] = total
    amounts = stacked(total)

    def step(at, i, carry):
        keep(at, w_ref[at, :] * (r_ref[at, :] - fast(rt_ref[at, :], amounts)), outs)
        return carry

    blocks_of(r_ref.shape[0], step, 0)
    send(edge_high_ref, edge_low_ref, outs)


def direct_first(near_ref, edge_high_ref, edge_low_ref, rt_ref, v_ref, *outs):
    total = summed(near_ref)
    outs[5][...] = total
    amounts = stacked(total)

    def step(at, i, carry):
        keep(at, v_ref[at, :] - fast(rt_ref[at, :], amounts), outs)
        return carry

    blocks_of(v_ref.shape[0], step, 0)
    send(edge_high_ref, edge_low_ref, outs)


def precondition_next(modes, near_ref, edge_high_ref, edge_low_ref, rt_ref, before_ref, norm_ref, r_ref, image_ref,
                      w_ref, *outs):
    size_ref, r_out_ref, step_ref = outs[5:]
    total = summed(near_ref)
    length = norm_ref[modes:modes + 1, :] / total[modes:modes + 1]
    step_ref[...] = length
    amounts = stacked(before_ref[...] - length * total)

    def step(at, i, size):
        residual = r_ref[at, :] - length * image_ref[at, :]
        r_out_ref[at, :] = residual
        weighted = w_ref[at, :] * residual
        keep(at, w_ref[at, :] * (residual - fast(rt_ref[at, :], amounts)), outs)
        return size + jnp.sum(weighted * residual, axis=0, keepdims=True)

    size_ref[...] = blocks_of(r_ref.shape[0], step, jnp.zeros((1, r_ref.shape[1]), F32))
    send(edge_high_ref, edge_low_ref, outs)


def direct_next(modes, near_ref, edge_high_ref, edge_low_ref, rt_ref, norm_ref, first_ref, v_ref, d_ref, *outs):
    total = summed(near_ref)
    outs[5][...] = total
    outs[6][0:1, :] = first_ref[modes:modes + 1, :]
    outs[6][1:2, :] = total[modes + 1:modes + 2]
    ratio = total[modes:modes + 1] / norm_ref[modes:modes + 1, :]
    amounts = stacked(total)

    def step(at, i, carry):
        update = v_ref[at, :] - fast(rt_ref[at, :], amounts)
        keep(at, update + ratio * d_ref[at, :], outs)
        return carry

    blocks_of(v_ref.shape[0], step, 0)
    send(edge_high_ref, edge_low_ref, outs)


def received(mate_ref, far_ref):
    return halves(jnp.concatenate([mate_ref[...], far_ref[...]], axis=0))


def pack_out(modes, pack_ref, sums, low_sums, first, second):
    part = sums[:TILE] + sums[TILE:] + low_sums[:TILE]
    row = lax.broadcasted_iota(jnp.int32, part.shape, 0)
    part = jnp.where(row == modes, first, jnp.where(row == modes + 1, second, part))
    for member in range(pack_ref.shape[0]):
        pack_ref[member] = part


def gather_modes(rigid_ref, value, i, sums, low_sums):
    zh, zl = halves(value)
    rigid = rigid_ref[i]
    return sums + fast(rigid, zh), low_sums + fast(rigid, zl)


def paired(value):
    high, low = halves(value)
    return jnp.concatenate([high.astype(F32), low.astype(F32)], axis=0).astype(BF16)


def folded(pair):
    return pair[:TILE] + pair[TILE:]


def prepare_body(modes, group, gap_in_ref, coarse_in_ref, rigid_in_ref, s_ref, mate_ref, far_ref, wide_ref,
                 gap_ref, coarse_raw_ref, rigid_raw_ref, coarse_ref, rigid_ref, sems):
    loads = [
        pltpu.make_async_copy(source_ref, target_ref, sems.at[number])
        for number, (source_ref, target_ref) in enumerate(
            ((gap_in_ref, gap_ref), (coarse_in_ref, coarse_raw_ref), (rigid_in_ref, rigid_raw_ref))
        )
    ]
    for load in loads:
        load.start()
    for load in loads:
        load.wait()
    for source_ref, tile_ref in ((coarse_raw_ref, coarse_ref), (rigid_raw_ref, rigid_ref)):
        tile_ref[...] = jnp.zeros_like(tile_ref)
        tile_ref[:modes, :] = source_ref[...]
    shared = s_ref.shape[1] // 2
    cases = gap_ref.shape[1]

    def step(at, i, sent):
        high, rest = halves(gap_ref[at, :])
        pick = s_ref[i]
        low = rest.astype(F32)
        tail = (gap_ref[at, :] - high.astype(F32) - low).astype(BF16)
        return sent + (fast(pick, high) + fast(pick, rest) + fast(pick, tail))

    sent = blocks_of(gap_ref.shape[0], step, jnp.zeros((2 * shared, cases), F32))
    mate_ref[:shared, :] = sent[:shared]
    far_ref[:shared, :] = sent[shared:]

    narrow, wide = 4 * group * modes, 4 * group * TILE
    column = lax.broadcasted_iota(jnp.int32, (narrow, wide), 1)
    source = (column // TILE) * modes + column % TILE
    source = jnp.where(column % TILE < modes, source, -1)
    widen = jnp.where(lax.broadcasted_iota(jnp.int32, (narrow, wide), 0) == source, 1.0, 0.0).astype(BF16)
    for part in range(coarse_ref.shape[1] // narrow):
        spread = folded(fast(paired(coarse_ref[:, part * narrow:(part + 1) * narrow]), widen))
        for piece in range(wide // cases):
            top = shared + TILE * (part * (wide // cases) + piece)
            value = spread[:, piece * cases:(piece + 1) * cases]
            mate_ref[top:top + TILE, :] = value
            far_ref[top:top + TILE, :] = value

    picked = jnp.zeros((2 * TILE, 2 * shared), F32)
    for i in range(s_ref.shape[0]):
        rigid = paired(rigid_ref[:, i * ROWS:(i + 1) * ROWS])
        wide_ref[i] = rigid
        picked = picked + lax.dot_general(
            rigid, s_ref[i], (((1,), (1,)), ((), ())), preferred_element_type=F32
        )
    picked = folded(picked)
    spare = jnp.zeros((TILE, cases - shared), F32)
    last = mate_ref.shape[0] - TILE
    mate_ref[last:, :] = jnp.concatenate([picked[:, :shared], spare], axis=1)
    far_ref[last:, :] = jnp.concatenate([picked[:, shared:], spare], axis=1)


def tile_body(modes, shared, own_ref, mate_ref, far_ref, out_ref):
    wide = out_ref.shape[2]
    row = lax.broadcasted_iota(jnp.int32, (TILE, wide), 0)
    column = lax.broadcasted_iota(jnp.int32, (TILE, wide), 1)
    ones = jnp.where((row >= modes) & (column % TILE == row), 1.0, 0.0)
    per_row = own_ref.shape[1] // wide
    for member in range(out_ref.shape[0]):
        top = shared + TILE * (member // per_row)
        left = wide * (member % per_row)
        at = (slice(top, top + TILE), slice(left, left + wide))
        out_ref[member, :TILE, :] = own_ref[at] + ones
        out_ref[member, TILE:2 * TILE, :] = mate_ref[at]
        out_ref[member, 2 * TILE:, :] = far_ref[at]


def start_body(modes, y_ref, mate_ref, far_ref, st_ref, w_ref, wide_ref, out_ref, pack_ref, tall_ref):
    shared = st_ref.shape[1] // 2
    cases = y_ref.shape[1]
    rows = jnp.concatenate([mate_ref[:shared, :], far_ref[:shared, :]], axis=0)
    rh, rest = halves(rows)
    rt = (rows - rh.astype(F32) - rest.astype(F32)).astype(BF16)
    last = mate_ref.shape[0] - TILE
    near_mate = paired(mate_ref[last:, :shared])
    near_far = paired(far_ref[last:, :shared])
    spare = jnp.zeros((TILE, ROWS), F32)

    def step(at, i, carry):
        size, sums, low_sums = carry
        place = st_ref[at, :]
        value = y_ref[at, :] + (fast(place, rh) + fast(place, rest) + fast(place, rt))
        out_ref[at, :] = value
        size = size + jnp.sum(w_ref[at, :] * value * value, axis=0, keepdims=True)

        def across(near, hot):
            return folded(lax.dot_general(near, hot, (((1,), (1,)), ((), ())), preferred_element_type=F32))

        own = folded(wide_ref[i].astype(F32))
        stack = jnp.concatenate(
            [own, across(near_mate, place[:, :shared]), across(near_far, place[:, shared:]), spare], axis=0
        )
        high, low = halves(stack)
        high, low = high.astype(F32), low.astype(F32)
        stack = jnp.concatenate([high, high, low, jnp.zeros_like(low)], axis=0)
        tall_ref[at, :] = stack.T.astype(BF16)
        return (size, *gather_modes(wide_ref, value, i, sums, low_sums))

    zeros = jnp.zeros((2 * TILE, cases), F32)
    size, sums, low_sums = blocks_of(y_ref.shape[0], step, (jnp.zeros((1, cases), F32), zeros, zeros))
    pack_out(modes, pack_ref, sums, low_sums, size, jnp.zeros_like(size))


def assemble_body(modes, weighted, sized, *refs):
    y_ref, mate_ref, far_ref, st_ref, rigid_ref, part_ref = refs[:6]
    w_ref = refs[6] if weighted else None
    size_ref = refs[6 + weighted] if sized else None
    out_ref, pack_ref = refs[6 + weighted + sized:]
    rh, rl = received(mate_ref, far_ref)

    def step(at, i, carry):
        place = st_ref[at, :]
        value = y_ref[at, :] + (fast(place, rh) + fast(place, rl))
        if weighted:
            value = w_ref[at, :] * value
        out_ref[at, :] = value
        return gather_modes(rigid_ref, value, i, *carry)

    zeros = jnp.zeros((2 * TILE, y_ref.shape[1]), F32)
    sums, low_sums = blocks_of(y_ref.shape[0], step, (zeros, zeros))
    part = part_ref[...]
    pack_out(modes, pack_ref, sums, low_sums, part, size_ref[...] if sized else jnp.zeros_like(part))


def block_body(block_ref, near_ref, out_ref):
    members, tile, cases = near_ref.shape
    high, low = halves(near_ref[...].reshape(members * tile, cases))
    outer, tall, wide = block_ref.shape
    block_high, block_low = halves(block_ref[...].reshape(outer * tall, wide))
    block = jnp.concatenate([block_high, block_high, block_low], axis=1)
    out = fast(block, jnp.concatenate([high, low, high], axis=0))
    out_ref[...] = out.reshape(out_ref.shape)


def finish_body(modes, q_ref, mate_ref, far_ref, st_ref, r_ref, first_ref, second_ref, step_first_ref, last_ref,
                bending_ref, multipliers_ref, residual_ref):
    rh, rl = received(mate_ref, far_ref)
    first = step_first_ref[...]
    second = last_ref[modes:modes + 1, :] / summed(bending_ref)

    def step(at, i, carry):
        place = st_ref[at, :]
        image = q_ref[at, :] + (fast(place, rh) + fast(place, rl))
        multipliers_ref[at, :] = first * first_ref[at, :] + second * second_ref[at, :]
        residual_ref[at, :] = r_ref[at, :] - second * image
        return carry

    blocks_of(q_ref.shape[0], step, 0)


def shards(dual_ops, boundary_solve_blocks, rigid_images, coarse_rows, gap_raw, row_maps):
    modes, local_rows = rigid_images.shape
    cases = gap_raw.shape[1]
    count = lax.axis_size(CLUSTER_SUB)
    outer, inner = lax.axis_size(OUTER), lax.axis_size(INNER)
    place = lax.axis_index(CLUSTER_SUB)
    even = place % 2 == 0
    inside = jnp.where((place > 0) & (place < count - 1), 1.0, 0.0).astype(F32)
    mate = jnp.where(even, row_maps[0, 1], row_maps[0, 0])
    far = jnp.where(even, row_maps[0, 0], row_maps[0, 1])
    shared = mate.shape[0]
    mate_pairs, far_pairs = matchings(count)

    def exchanged(to_mate, to_far):
        from_far = matched(to_far, far_pairs)
        from_mate = matched(to_mate, mate_pairs)
        return from_mate, from_far

    picks = jnp.concatenate([mate, far])
    live = jnp.concatenate([jnp.ones((shared,), F32), jnp.full((shared,), inside)])
    blocks = (local_rows // ROWS, 2 * shared, ROWS)
    numbers = lax.broadcasted_iota(jnp.int32, blocks, 0) * ROWS + lax.broadcasted_iota(jnp.int32, blocks, 2)
    selector = jnp.where(picks[None, :, None] == numbers, live[None, :, None], 0.0).astype(BF16)
    placer = jnp.where(
        picks[None, :] == lax.broadcasted_iota(jnp.int32, (local_rows, 2 * shared), 0), live[None, :], 0.0
    )
    weights = jnp.broadcast_to(1.0 - 0.5 * jnp.sum(placer, axis=1, keepdims=True), (local_rows, cases))
    placer = placer.astype(BF16)

    field = (local_rows, cases)
    edge = (shared, cases)
    row = (1, cases)
    rows_out = (3 * TILE, cases)
    pack_shape = (inner, TILE, cases)
    big = 6 * local_rows * local_rows * cases
    light = 4 * local_rows * cases * 2 * shared
    moved = 4 * local_rows * (local_rows + 3 * cases)

    def shaped(shape, dtype):
        return jax.ShapeDtypeStruct(shape, dtype)

    payload = (shared + TILE * (outer * inner * TILE // cases) + TILE, cases)
    to_mate, to_far, rigid_wide = call(
        functools.partial(prepare_body, modes, inner),
        [payload, payload, shaped((local_rows // ROWS, 2 * TILE, ROWS), BF16)],
        [
            pltpu.VMEM(field, F32),
            pltpu.VMEM(coarse_rows.shape, F32),
            pltpu.VMEM(rigid_images.shape, F32),
            pltpu.VMEM((TILE, coarse_rows.shape[1]), F32),
            pltpu.VMEM((TILE, local_rows), F32),
            pltpu.SemaphoreType.DMA((3,)),
        ],
        light, 8 * local_rows * cases, outside=3, limit=LARGE_LIMIT,
    )(gap_raw, coarse_rows, rigid_images, selector)
    from_mate, from_far = exchanged(to_mate, to_far)
    edges = [
        call(pick_body, [shaped((2 * shared, local_rows), BF16)] * 2, [], light, 4 * local_rows * local_rows)(m, selector)
        for m in (boundary_solve_blocks, dual_ops)
    ]
    from_mate, from_far, placer, weights, edges = lax.optimization_barrier(
        (from_mate, from_far, placer, weights, edges)
    )
    [block] = call(
        functools.partial(tile_body, modes, shared), [(outer, 3 * TILE, inner * TILE)], [], 1, 8 * local_rows
    )(to_mate, from_mate, from_far)
    block = swap(block, OUTER)
    block, from_mate, from_far, placer, weights, edges = lax.optimization_barrier(
        (block, from_mate, from_far, placer, weights, edges)
    )

    def coarse(pack):
        near = swap(pack, INNER)
        [rows] = call(block_body, [(outer, 3 * TILE, cases)], [], 6 * outer * 3 * TILE * inner * TILE * cases,
                      4 * outer * 4 * TILE * cases)(block, near)
        return swap(rows, OUTER)

    def assemble(weighted, sized, *operands):
        body = functools.partial(assemble_body, modes, weighted, sized)
        return call(body, [field, pack_shape], [], light, 12 * local_rows * cases)(*operands)

    residual, pack, rigid_tall = call(
        functools.partial(start_body, modes), [field, pack_shape, shaped((local_rows, 128), BF16)], [], light,
        12 * local_rows * cases,
    )(gap_raw, from_mate, from_far, placer, weights, rigid_wide)
    sent = [edge, edge, field, shaped(field, BF16), shaped(field, BF16)]

    def advance(body, extra, near, which, *operands, parts=row):
        to_mate, to_far, x, high, low, *rest = call(
            body, sent + extra, [], light, 12 * local_rows * cases
        )(near, *edges[which], rigid_tall, *operands)
        out, part = call(multiply_body, [field, parts], [], big, moved)(
            (boundary_solve_blocks, dual_ops)[which], x, high, low
        )
        return out, exchanged(to_mate, to_far), part, x, *rest

    near = coarse(pack)
    out, received_rows, part, _, amounts = advance(precondition_first, [rows_out], near, 0, residual, weights)
    smoothed, pack = assemble(True, False, out, *received_rows, placer, rigid_wide, part, weights)
    near = coarse(pack)
    out, received_rows, part, direction_first, total = advance(direct_first, [rows_out], near, 1, smoothed)
    image, pack = assemble(False, False, out, *received_rows, placer, rigid_wide, part)
    near = coarse(pack)
    out, received_rows, part, _, size, residual, step_first = advance(
        functools.partial(precondition_next, modes), [row, field, row], near, 0, amounts, total, residual, image, weights
    )
    smoothed, pack = assemble(True, True, out, *received_rows, placer, rigid_wide, part, weights, size)
    near = coarse(pack)
    out, (from_mate, from_far), part, direction, last, norms = advance(
        functools.partial(direct_next, modes), [rows_out, (2, cases)], near, 1, total, amounts, smoothed, direction_first,
        parts=(inner, 1, cases),
    )
    part, norms, from_mate, from_far = lax.optimization_barrier((part, norms, from_mate, from_far))
    [part] = call(relay_body, [(outer, 1, cases)], [], 1, 4 * outer * cases)(swap(part, INNER))
    bending = swap(part, OUTER)
    multipliers, residual = call(functools.partial(finish_body, modes), [field, field], [], light, 24 * local_rows * cases)(
        out, from_mate, from_far, placer, residual, direction_first, direction, step_first, last, bending
    )
    return (multipliers, residual, norms)


def solution(mesh):
    devices = mesh.devices
    x, sub = devices.shape
    split = Mesh(devices.reshape(x, 4, sub // 8, 2), CLUSTER_SUB)
    in_specs = (P(CLUSTER_SUB, None),) * 5 + (P(CLUSTER_SUB, None, None),)
    out_specs = (P(CLUSTER_SUB, None), P(CLUSTER_SUB, None), P())
    return jax.shard_map(
        shards, mesh=split, in_specs=in_specs, out_specs=out_specs, check_vma=False
    )
```

```python
import functools

import jax
import jax.numpy as jnp
from jax import lax
from jax.experimental import pallas as pl
from jax.experimental.pallas import tpu as pltpu
from jax.sharding import Mesh
from jax.sharding import PartitionSpec as P

CLUSTER_SUB = ("cluster", "sub_0", "sub_1", "sub_2")
OUTER = ("cluster", "sub_0")
INNER = ("sub_1", "sub_2")
TILE = 8
ROWS = 256
VMEM_LIMIT = 24 * 1024 * 1024

F32 = jnp.float32
BF16 = jnp.bfloat16


def fast(a, b):
    return jnp.dot(a, b, preferred_element_type=F32)


def halves(value):
    high = value.astype(BF16)
    return high, (value - high.astype(F32)).astype(BF16)


def swap(blocks, axis):
    return lax.all_to_all(blocks, axis, split_axis=0, concat_axis=0, tiled=True)


def matched(value, pairs):
    return lax.ppermute(value, CLUSTER_SUB, pairs)


def matchings(count):
    near = [(i, i ^ 1) for i in range(count)]
    far = [(i, (((i + 1) ^ 1) - 1) % count) for i in range(count)]
    return near, far


def call(body, out_shapes, scratch, flops, moved):
    def run(*operands):
        return pl.pallas_call(
            body,
            out_shape=[s if hasattr(s, "dtype") else jax.ShapeDtypeStruct(s, F32) for s in out_shapes],
            in_specs=[pl.BlockSpec(memory_space=pltpu.VMEM)] * len(operands),
            out_specs=[pl.BlockSpec(memory_space=pltpu.VMEM)] * len(out_shapes),
            scratch_shapes=scratch,
            compiler_params=pltpu.CompilerParams(vmem_limit_bytes=VMEM_LIMIT),
            cost_estimate=pl.CostEstimate(flops=flops, bytes_accessed=moved, transcendentals=0),
        )(*operands)

    return run


def summed(near_ref):
    total = near_ref[0]
    for member in range(1, near_ref.shape[0]):
        total = total + near_ref[member]
    return total


def stacked(amounts):
    spare = jnp.zeros((TILE, amounts.shape[1]), F32)
    high, low = halves(jnp.concatenate([amounts, spare], axis=0))
    return jnp.concatenate([high, low, high, jnp.zeros_like(high)], axis=0)


def blocks_of(rows, body, start):
    return lax.fori_loop(0, rows // ROWS, lambda i, c: body(pl.ds(pl.multiple_of(i * ROWS, ROWS), ROWS), i, c), start)


def pick_body(m_ref, s_ref, high_ref, low_ref):
    def step(j, carry):
        at = pl.ds(pl.multiple_of(j * ROWS, ROWS), ROWS)
        rows = rest = jnp.zeros((s_ref.shape[1], ROWS), F32)
        for i in range(s_ref.shape[0]):
            high, low = halves(m_ref[i * ROWS:(i + 1) * ROWS, at])
            pick = s_ref[i]
            rows, rest = rows + fast(pick, high), rest + fast(pick, low)
        high_ref[:, at], low_ref[:, at] = rows.astype(BF16), rest.astype(BF16)
        return carry

    lax.fori_loop(0, m_ref.shape[1] // ROWS, step, 0)


def multiply_body(m_ref, x_ref, high_ref, low_ref, out_ref, part_ref):
    xh, xl = high_ref[...], low_ref[...]

    def step(at, i, part):
        mh, ml = halves(m_ref[at, :])
        out = fast(mh, xh) + fast(mh, xl) + fast(ml, xh)
        out_ref[at, :] = out
        return part + jnp.sum(x_ref[at, :] * out, axis=0, keepdims=True)

    part = blocks_of(out_ref.shape[0], step, jnp.zeros((1, out_ref.shape[1]), F32))
    copied(part_ref, part)


def copied(ref, row):
    if len(ref.shape) == 2:
        ref[...] = row
        return
    for member in range(ref.shape[0]):
        ref[member] = row


def relay_body(near_ref, out_ref):
    copied(out_ref, summed(near_ref))


def keep(at, x, outs):
    x_ref, high_ref, low_ref = outs[2:5]
    x_ref[at, :] = x
    high_ref[at, :], low_ref[at, :] = halves(x)


def send(edge_high_ref, edge_low_ref, outs):
    mate_ref, far_ref, _, high_ref, low_ref = outs[:5]
    xh, xl, mh = high_ref[...], low_ref[...], edge_high_ref[...]
    sent = fast(mh, xh) + fast(mh, xl) + fast(edge_low_ref[...], xh)
    shared = mate_ref.shape[0]
    mate_ref[...] = sent[:shared]
    far_ref[...] = sent[shared:]


def precondition_first(near_ref, edge_high_ref, edge_low_ref, rt_ref, r_ref, w_ref, *outs):
    total = summed(near_ref)
    outs[5][...] = total
    amounts = stacked(total)

    def step(at, i, carry):
        keep(at, w_ref[at, :] * (r_ref[at, :] - fast(rt_ref[at, :], amounts)), outs)
        return carry

    blocks_of(r_ref.shape[0], step, 0)
    send(edge_high_ref, edge_low_ref, outs)


def direct_first(near_ref, edge_high_ref, edge_low_ref, rt_ref, v_ref, *outs):
    total = summed(near_ref)
    outs[5][...] = total
    amounts = stacked(total)

    def step(at, i, carry):
        keep(at, v_ref[at, :] - fast(rt_ref[at, :], amounts), outs)
        return carry

    blocks_of(v_ref.shape[0], step, 0)
    send(edge_high_ref, edge_low_ref, outs)


def precondition_next(modes, near_ref, edge_high_ref, edge_low_ref, rt_ref, before_ref, norm_ref, r_ref, image_ref,
                      w_ref, *outs):
    size_ref, r_out_ref, step_ref = outs[5:]
    total = summed(near_ref)
    length = norm_ref[modes:modes + 1, :] / total[modes:modes + 1]
    step_ref[...] = length
    amounts = stacked(before_ref[...] - length * total)

    def step(at, i, size):
        residual = r_ref[at, :] - length * image_ref[at, :]
        r_out_ref[at, :] = residual
        weighted = w_ref[at, :] * residual
        keep(at, w_ref[at, :] * (residual - fast(rt_ref[at, :], amounts)), outs)
        return size + jnp.sum(weighted * residual, axis=0, keepdims=True)

    size_ref[...] = blocks_of(r_ref.shape[0], step, jnp.zeros((1, r_ref.shape[1]), F32))
    send(edge_high_ref, edge_low_ref, outs)


def direct_next(modes, near_ref, edge_high_ref, edge_low_ref, rt_ref, norm_ref, first_ref, v_ref, d_ref, *outs):
    total = summed(near_ref)
    outs[5][...] = total
    outs[6][0:1, :] = first_ref[modes:modes + 1, :]
    outs[6][1:2, :] = total[modes + 1:modes + 2]
    ratio = total[modes:modes + 1] / norm_ref[modes:modes + 1, :]
    amounts = stacked(total)

    def step(at, i, carry):
        update = v_ref[at, :] - fast(rt_ref[at, :], amounts)
        keep(at, update + ratio * d_ref[at, :], outs)
        return carry

    blocks_of(v_ref.shape[0], step, 0)
    send(edge_high_ref, edge_low_ref, outs)


def received(mate_ref, far_ref):
    return halves(jnp.concatenate([mate_ref[...], far_ref[...]], axis=0))


def pack_out(modes, pack_ref, sums, low_sums, first, second):
    part = sums[:TILE] + sums[TILE:] + low_sums[:TILE]
    row = lax.broadcasted_iota(jnp.int32, part.shape, 0)
    part = jnp.where(row == modes, first, jnp.where(row == modes + 1, second, part))
    for member in range(pack_ref.shape[0]):
        pack_ref[member] = part


def gather_modes(rigid_ref, value, i, sums, low_sums):
    zh, zl = halves(value)
    rigid = rigid_ref[i]
    return sums + fast(rigid, zh), low_sums + fast(rigid, zl)


def paired(value):
    high, low = halves(value)
    return jnp.concatenate([high.astype(F32), low.astype(F32)], axis=0).astype(BF16)


def folded(pair):
    return pair[:TILE] + pair[TILE:]


def prepare_body(modes, group, gap_ref, coarse_ref, rigid_ref, s_ref, mate_ref, far_ref, wide_ref):
    shared = s_ref.shape[1] // 2
    cases = gap_ref.shape[1]

    def step(at, i, sent):
        high, rest = halves(gap_ref[at, :])
        pick = s_ref[i]
        low = rest.astype(F32)
        tail = (gap_ref[at, :] - high.astype(F32) - low).astype(BF16)
        return sent + (fast(pick, high) + fast(pick, rest) + fast(pick, tail))

    sent = blocks_of(gap_ref.shape[0], step, jnp.zeros((2 * shared, cases), F32))
    mate_ref[:shared, :] = sent[:shared]
    far_ref[:shared, :] = sent[shared:]

    narrow, wide = 4 * group * modes, 4 * group * TILE
    column = lax.broadcasted_iota(jnp.int32, (narrow, wide), 1)
    source = (column // TILE) * modes + column % TILE
    source = jnp.where(column % TILE < modes, source, -1)
    widen = jnp.where(lax.broadcasted_iota(jnp.int32, (narrow, wide), 0) == source, 1.0, 0.0).astype(BF16)
    for part in range(coarse_ref.shape[1] // narrow):
        spread = folded(fast(paired(coarse_ref[:, part * narrow:(part + 1) * narrow]), widen))
        for piece in range(wide // cases):
            top = shared + TILE * (part * (wide // cases) + piece)
            value = spread[:, piece * cases:(piece + 1) * cases]
            mate_ref[top:top + TILE, :] = value
            far_ref[top:top + TILE, :] = value

    picked = jnp.zeros((2 * TILE, 2 * shared), F32)
    for i in range(s_ref.shape[0]):
        rigid = paired(rigid_ref[:, i * ROWS:(i + 1) * ROWS])
        wide_ref[i] = rigid
        picked = picked + lax.dot_general(
            rigid, s_ref[i], (((1,), (1,)), ((), ())), preferred_element_type=F32
        )
    picked = folded(picked)
    spare = jnp.zeros((TILE, cases - shared), F32)
    last = mate_ref.shape[0] - TILE
    mate_ref[last:, :] = jnp.concatenate([picked[:, :shared], spare], axis=1)
    far_ref[last:, :] = jnp.concatenate([picked[:, shared:], spare], axis=1)


def tile_body(modes, shared, own_ref, mate_ref, far_ref, out_ref):
    wide = out_ref.shape[2]
    row = lax.broadcasted_iota(jnp.int32, (TILE, wide), 0)
    column = lax.broadcasted_iota(jnp.int32, (TILE, wide), 1)
    ones = jnp.where((row >= modes) & (column % TILE == row), 1.0, 0.0)
    per_row = own_ref.shape[1] // wide
    for member in range(out_ref.shape[0]):
        top = shared + TILE * (member // per_row)
        left = wide * (member % per_row)
        at = (slice(top, top + TILE), slice(left, left + wide))
        out_ref[member, :TILE, :] = own_ref[at] + ones
        out_ref[member, TILE:2 * TILE, :] = mate_ref[at]
        out_ref[member, 2 * TILE:, :] = far_ref[at]


def start_body(modes, y_ref, mate_ref, far_ref, st_ref, w_ref, wide_ref, out_ref, pack_ref, tall_ref):
    shared = st_ref.shape[1] // 2
    cases = y_ref.shape[1]
    rows = jnp.concatenate([mate_ref[:shared, :], far_ref[:shared, :]], axis=0)
    rh, rest = halves(rows)
    rt = (rows - rh.astype(F32) - rest.astype(F32)).astype(BF16)
    last = mate_ref.shape[0] - TILE
    near_mate = paired(mate_ref[last:, :shared])
    near_far = paired(far_ref[last:, :shared])
    spare = jnp.zeros((TILE, ROWS), F32)

    def step(at, i, carry):
        size, sums, low_sums = carry
        place = st_ref[at, :]
        value = y_ref[at, :] + (fast(place, rh) + fast(place, rest) + fast(place, rt))
        out_ref[at, :] = value
        size = size + jnp.sum(w_ref[at, :] * value * value, axis=0, keepdims=True)

        def across(near, hot):
            return folded(lax.dot_general(near, hot, (((1,), (1,)), ((), ())), preferred_element_type=F32))

        own = folded(wide_ref[i].astype(F32))
        stack = jnp.concatenate(
            [own, across(near_mate, place[:, :shared]), across(near_far, place[:, shared:]), spare], axis=0
        )
        high, low = halves(stack)
        high, low = high.astype(F32), low.astype(F32)
        stack = jnp.concatenate([high, high, low, jnp.zeros_like(low)], axis=0)
        tall_ref[at, :] = stack.T.astype(BF16)
        return (size, *gather_modes(wide_ref, value, i, sums, low_sums))

    zeros = jnp.zeros((2 * TILE, cases), F32)
    size, sums, low_sums = blocks_of(y_ref.shape[0], step, (jnp.zeros((1, cases), F32), zeros, zeros))
    pack_out(modes, pack_ref, sums, low_sums, size, jnp.zeros_like(size))


def assemble_body(modes, weighted, sized, *refs):
    y_ref, mate_ref, far_ref, st_ref, rigid_ref, part_ref = refs[:6]
    w_ref = refs[6] if weighted else None
    size_ref = refs[6 + weighted] if sized else None
    out_ref, pack_ref = refs[6 + weighted + sized:]
    rh, rl = received(mate_ref, far_ref)

    def step(at, i, carry):
        place = st_ref[at, :]
        value = y_ref[at, :] + (fast(place, rh) + fast(place, rl))
        if weighted:
            value = w_ref[at, :] * value
        out_ref[at, :] = value
        return gather_modes(rigid_ref, value, i, *carry)

    zeros = jnp.zeros((2 * TILE, y_ref.shape[1]), F32)
    sums, low_sums = blocks_of(y_ref.shape[0], step, (zeros, zeros))
    part = part_ref[...]
    pack_out(modes, pack_ref, sums, low_sums, part, size_ref[...] if sized else jnp.zeros_like(part))


def block_body(block_ref, near_ref, out_ref):
    members, tile, cases = near_ref.shape
    high, low = halves(near_ref[...].reshape(members * tile, cases))
    outer, tall, wide = block_ref.shape
    block_high, block_low = halves(block_ref[...].reshape(outer * tall, wide))
    block = jnp.concatenate([block_high, block_high, block_low], axis=1)
    out = fast(block, jnp.concatenate([high, low, high], axis=0))
    out_ref[...] = out.reshape(out_ref.shape)


def finish_body(modes, q_ref, mate_ref, far_ref, st_ref, r_ref, first_ref, second_ref, step_first_ref, last_ref,
                bending_ref, multipliers_ref, residual_ref):
    rh, rl = received(mate_ref, far_ref)
    first = step_first_ref[...]
    second = last_ref[modes:modes + 1, :] / summed(bending_ref)

    def step(at, i, carry):
        place = st_ref[at, :]
        image = q_ref[at, :] + (fast(place, rh) + fast(place, rl))
        multipliers_ref[at, :] = first * first_ref[at, :] + second * second_ref[at, :]
        residual_ref[at, :] = r_ref[at, :] - second * image
        return carry

    blocks_of(q_ref.shape[0], step, 0)


def shards(dual_ops, boundary_solve_blocks, rigid_images, coarse_rows, gap_raw, row_maps):
    modes, local_rows = rigid_images.shape
    cases = gap_raw.shape[1]
    count = lax.axis_size(CLUSTER_SUB)
    outer, inner = lax.axis_size(OUTER), lax.axis_size(INNER)
    place = lax.axis_index(CLUSTER_SUB)
    even = place % 2 == 0
    inside = jnp.where((place > 0) & (place < count - 1), 1.0, 0.0).astype(F32)
    mate = jnp.where(even, row_maps[0, 1], row_maps[0, 0])
    far = jnp.where(even, row_maps[0, 0], row_maps[0, 1])
    shared = mate.shape[0]
    mate_pairs, far_pairs = matchings(count)

    def exchanged(to_mate, to_far):
        from_far = matched(to_far, far_pairs)
        from_mate = matched(to_mate, mate_pairs)
        return from_mate, from_far

    picks = jnp.concatenate([mate, far])
    live = jnp.concatenate([jnp.ones((shared,), F32), jnp.full((shared,), inside)])
    blocks = (local_rows // ROWS, 2 * shared, ROWS)
    numbers = lax.broadcasted_iota(jnp.int32, blocks, 0) * ROWS + lax.broadcasted_iota(jnp.int32, blocks, 2)
    selector = jnp.where(picks[None, :, None] == numbers, live[None, :, None], 0.0).astype(BF16)
    placer = jnp.where(
        picks[None, :] == lax.broadcasted_iota(jnp.int32, (local_rows, 2 * shared), 0), live[None, :], 0.0
    )
    weights = jnp.broadcast_to(1.0 - 0.5 * jnp.sum(placer, axis=1, keepdims=True), (local_rows, cases))
    placer = placer.astype(BF16)

    field = (local_rows, cases)
    edge = (shared, cases)
    row = (1, cases)
    rows_out = (3 * TILE, cases)
    pack_shape = (inner, TILE, cases)
    big = 6 * local_rows * local_rows * cases
    light = 4 * local_rows * cases * 2 * shared
    moved = 4 * local_rows * (local_rows + 3 * cases)

    def shaped(shape, dtype):
        return jax.ShapeDtypeStruct(shape, dtype)

    pad = ((0, TILE - modes), (0, 0))
    payload = (shared + TILE * (outer * inner * TILE // cases) + TILE, cases)
    to_mate, to_far, rigid_wide = call(
        functools.partial(prepare_body, modes, inner),
        [payload, payload, shaped((local_rows // ROWS, 2 * TILE, ROWS), BF16)], [], light, 8 * local_rows * cases,
    )(gap_raw, jnp.pad(coarse_rows, pad), jnp.pad(rigid_images, pad), selector)
    from_mate, from_far = exchanged(to_mate, to_far)
    edges = [
        call(pick_body, [shaped((2 * shared, local_rows), BF16)] * 2, [], light, 4 * local_rows * local_rows)(m, selector)
        for m in (boundary_solve_blocks, dual_ops)
    ]
    from_mate, from_far, placer, weights, edges = lax.optimization_barrier(
        (from_mate, from_far, placer, weights, edges)
    )
    [block] = call(
        functools.partial(tile_body, modes, shared), [(outer, 3 * TILE, inner * TILE)], [], 1, 8 * local_rows
    )(to_mate, from_mate, from_far)
    block = swap(block, OUTER)
    block, from_mate, from_far, placer, weights, edges = lax.optimization_barrier(
        (block, from_mate, from_far, placer, weights, edges)
    )

    def coarse(pack):
        near = swap(pack, INNER)
        [rows] = call(block_body, [(outer, 3 * TILE, cases)], [], 6 * outer * 3 * TILE * inner * TILE * cases,
                      4 * outer * 4 * TILE * cases)(block, near)
        return swap(rows, OUTER)

    def assemble(weighted, sized, *operands):
        body = functools.partial(assemble_body, modes, weighted, sized)
        return call(body, [field, pack_shape], [], light, 12 * local_rows * cases)(*operands)

    residual, pack, rigid_tall = call(
        functools.partial(start_body, modes), [field, pack_shape, shaped((local_rows, 128), BF16)], [], light,
        12 * local_rows * cases,
    )(gap_raw, from_mate, from_far, placer, weights, rigid_wide)
    sent = [edge, edge, field, shaped(field, BF16), shaped(field, BF16)]

    def advance(body, extra, near, which, *operands, parts=row):
        to_mate, to_far, x, high, low, *rest = call(
            body, sent + extra, [], light, 12 * local_rows * cases
        )(near, *edges[which], rigid_tall, *operands)
        out, part = call(multiply_body, [field, parts], [], big, moved)(
            (boundary_solve_blocks, dual_ops)[which], x, high, low
        )
        return out, exchanged(to_mate, to_far), part, x, *rest

    near = coarse(pack)
    out, received_rows, part, _, amounts = advance(precondition_first, [rows_out], near, 0, residual, weights)
    smoothed, pack = assemble(True, False, out, *received_rows, placer, rigid_wide, part, weights)
    near = coarse(pack)
    out, received_rows, part, direction_first, total = advance(direct_first, [rows_out], near, 1, smoothed)
    image, pack = assemble(False, False, out, *received_rows, placer, rigid_wide, part)
    near = coarse(pack)
    out, received_rows, part, _, size, residual, step_first = advance(
        functools.partial(precondition_next, modes), [row, field, row], near, 0, amounts, total, residual, image, weights
    )
    smoothed, pack = assemble(True, True, out, *received_rows, placer, rigid_wide, part, weights, size)
    near = coarse(pack)
    out, (from_mate, from_far), part, direction, last, norms = advance(
        functools.partial(direct_next, modes), [rows_out, (2, cases)], near, 1, total, amounts, smoothed, direction_first,
        parts=(inner, 1, cases),
    )
    part, norms, from_mate, from_far = lax.optimization_barrier((part, norms, from_mate, from_far))
    [part] = call(relay_body, [(outer, 1, cases)], [], 1, 4 * outer * cases)(swap(part, INNER))
    bending = swap(part, OUTER)
    multipliers, residual = call(functools.partial(finish_body, modes), [field, field], [], light, 24 * local_rows * cases)(
        out, from_mate, from_far, placer, residual, direction_first, direction, step_first, last, bending
    )
    return (multipliers, residual, norms)


def solution(mesh):
    devices = mesh.devices
    x, sub = devices.shape
    split = Mesh(devices.reshape(x, 4, sub // 8, 2), CLUSTER_SUB)
    in_specs = (P(CLUSTER_SUB, None),) * 5 + (P(CLUSTER_SUB, None, None),)
    out_specs = (P(CLUSTER_SUB, None), P(CLUSTER_SUB, None), P())
    return jax.shard_map(
        shards, mesh=split, in_specs=in_specs, out_specs=out_specs, check_vma=False
    )
```
